128 devices in a mesh: prow: 8 (over x, z_lo), pcol: 16 (over z_hi, y, core).
Axes of the slice: x: 4, y: 4, z: 4 (z_hi: 2, z_lo: 2; z = z_hi * 2 + z_lo), core: 2. Of those that a mesh axis runs over, the one named last changes fastest.
Arguments:
- ancestor_inverse: float32 [4096, 4096], P('prow', 'pcol'), may hold values from -6 to 6
- lower_panel: float32 [4096, 2, 2048], P('prow'), may hold values from -0.09375 to 0.09375
- pivot_inverse: float32 [2, 2048, 2048], P(None, 'pcol', 'prow'), may hold values from -6 to 6
- structure: int32 [2, 64], replicated, may hold values from 0 to 1, as said below
Outputs:
- column_blocks: float32 [4096, 2, 2048], P(('prow', 'pcol'))
- diagonal_blocks: float32 [2, 2048, 2048], P(None, 'pcol', 'prow')
The draws below stay inside these ranges and needn't reach their ends.
Inputs may be any that keep to these rules, and one draw needn't show every extreme that they name: structure[k, b] is 1 when ancestor rows 64 * b to 64 * b + 63 belong to supernode k's structure, else 0; the last block belongs to every supernode.
All inputs are finite; a program needn't handle non-finite values.
Results may differ from the reference program's by a relative error of at most 0.000082.
Values sent between devices are 32-bit elements; how exact they have to be, the bound alone decides.
A program may use at most 128 MiB of HBM per device.

```python
import jax
import jax.numpy as jnp
from jax import lax

S = 2048
NSUP = 2
BLK = 64
M = 4096
NBLK = 64


def draw_structure(key, part):
    blocks = jnp.arange(NBLK, dtype=jnp.int32)[None, :]
    rolled = jax.random.randint(key, (NSUP, NBLK), 0, 5 * NBLK // 4 + 1)
    present = (rolled < blocks + NBLK // 4 + 1) | (blocks == NBLK - 1)
    return present.astype(jnp.int32)


def level_of(rng, extent, split, least, top_value):
    level, own = 1.0, jax.random.fold_in(rng, 6)
    for dim, shards_of in split:
        steps = jnp.exp(jax.random.uniform(jax.random.fold_in(own, dim), (shards_of,), jnp.float32, least / len(split), top_value / len(split)))
        level = level * jnp.repeat(steps, extent[dim] // shards_of).reshape([-1 if axis == dim else 1 for axis in range(len(extent))])
    return level


def normal_values(own_key, extent, deviation, limit, cuts=(), kind=jnp.bfloat16):
    entries = deviation * jax.random.normal(own_key, extent, jnp.float32)
    if cuts:
        entries = entries * level_of(own_key, extent, cuts, -0.22, 0.18)
    return jnp.clip(entries, -limit, limit).astype(kind)


def setup_inputs(seed: int = 0) -> dict:
    key_of = jax.random.split(jax.random.key(seed), 5)
    return {
        "ancestor_inverse": normal_values(key_of[0], (M, M), 1.0, 6.0, ((0, 8), (1, 16)), jnp.float32),
        "lower_panel": normal_values(key_of[1], (M, NSUP, S), M ** -0.5, 0.09375, ((0, 8),), jnp.float32),
        "pivot_inverse": normal_values(key_of[2], (NSUP, S, S), 1.0, 6.0, ((1, 16), (2, 8)), jnp.float32),
        "structure": draw_structure(jax.random.fold_in(key_of[4], 71), 0),
    }


def reference(ancestor_inverse, lower_panel, pivot_inverse, structure):
    blocks = jnp.arange(M, dtype=jnp.int32) // BLK
    onehot = (blocks[:, None] == jnp.arange(NBLK, dtype=jnp.int32)[None, :]).astype(jnp.float32)
    row_mask = jnp.dot(onehot, structure.astype(jnp.float32).T, precision=lax.Precision.HIGHEST)
    masked = lower_panel * row_mask[:, :, None]
    flat = masked.reshape(M, NSUP * S)
    product = jnp.dot(ancestor_inverse, flat, precision=lax.Precision.HIGHEST).reshape(M, NSUP, S)
    column_blocks = -row_mask[:, :, None] * product
    diagonal_blocks = pivot_inverse - jnp.einsum("aks,akt->kst", masked, column_blocks, precision=lax.Precision.HIGHEST)
    return column_blocks, diagonal_blocks
```

```python
import functools

import jax
import jax.numpy as jnp
from jax import lax
from jax.experimental import pallas as pl
from jax.experimental.pallas import tpu as pltpu
from jax.sharding import PartitionSpec as P

MESH = pl.DeviceIdType.MESH
F32 = jnp.float32
BF16 = jnp.bfloat16
S = 2048
NSUP = 2
BLK = 64
NX, NY, NZ = 4, 4, 4
NR, NC = 8, 16
W = 512
NCH = NSUP * S // W
PER_K = S // W
T = S // NC


def split(v):
    hi = v.astype(BF16)
    return hi, (v - hi.astype(F32)).astype(BF16)


def dot3(ahi, alo, bhi, blo):
    dot = functools.partial(jnp.dot, preferred_element_type=F32)
    return dot(ahi, bhi) + (dot(ahi, blo) + dot(alo, bhi))


def kernel(
    a_hbm, l_hbm, piv, structure, out_c, out_d,
    lst, xhi, xlo, abuf, ahi, alo, ybuf, zr, xo, xf, cbuf, dbuf, dxo, dxf, dsum, dfin,
    l_sem, a_send, a_recv, z_send, z_recv, xo_send, xo_recv, xf_send, xf_recv,
    c_send, c_recv, dxo_send, dxo_recv, dxf_send, dxf_recv, d_send, d_recv,
):
    pr, pc = lax.axis_index("prow"), lax.axis_index("pcol")
    rem, div = lax.rem, lax.div
    x, zl = div(pr, 2), rem(pr, 2)
    zh, rest = div(pc, 8), rem(pc, 8)
    z = 2 * zh + zl
    home, side = div(pc, 2), rem(pc, 2)

    def at_z(zz):
        return (x * 2 + rem(zz, 2), div(zz, 2) * 8 + rest)

    def at_x(xx):
        return (xx * 2 + zl, pc)

    z_down, z_up = at_z(rem(z + 3, 4)), at_z(rem(z + 1, 4))
    x_next, x_prev, x_far = rem(x + 1, 4), rem(x + 3, 4), rem(x + 2, 4)
    right, left = at_x(x_next), at_x(x_prev)
    is_home = home == pr

    def remote(src, dst, send, recv, device):
        return pltpu.make_async_remote_copy(
            src_ref=src, dst_ref=dst, send_sem=send, recv_sem=recv,
            device_id=device, device_id_type=MESH,
        )

    def await_bytes(ref, sem):
        pltpu.make_async_copy(ref, ref, sem).wait()

    rows = S * NSUP * BLK // 128
    l_copies = [
        pltpu.make_async_copy(
            l_hbm.at[pl.ds(i * rows, rows)], lst.at[pl.ds(i * rows, rows)], l_sem.at[i]
        )
        for i in range(NR)
    ]
    for copy in l_copies:
        copy.start()

    barrier = pltpu.get_barrier_semaphore()

    def greet(device):
        pl.semaphore_signal(barrier, inc=1, device_id=device, device_id_type=MESH)

    for device in (z_down, z_up, right, left):
        greet(device)
    for j in range(1, NC):
        greet((pr, rem(pc + j, NC)))
    for e in range(2):
        for j in range(1, NR):
            greet((rem(pr + j, NR), 2 * pr + e))

        @pl.when(2 * pr + e != pc)
        def _():
            greet((pr, 2 * pr + e))

    pl.semaphore_wait(barrier, jnp.where(is_home, 34, 35))

    home_zl = rem(home, 2)
    same = home_zl == zl

    def send_a(j):
        q = rem(pc + j, NC)
        z0 = 2 * div(q, 8) + zl
        for h in range(2):
            zt = rem(z0 + (1 if h == 0 else 3), 4)
            qt = jnp.where(same, q, div(zt, 2) * 8 + rem(q, 8))
            row = jnp.where(same, 128 + x * 32 + h * 16, h * 64 + x * 16)
            src = a_hbm.at[pl.ds(pl.multiple_of(q * 32 + h * 16, 16), 16)]
            dst = abuf.at[pl.ds(pl.multiple_of(row, 16), 16), pl.ds(pl.multiple_of(side * 256, 256), 256)]
            yield src, dst, (home, qt)

    for src, dst, device in send_a(0):
        @pl.when(is_home)
        def _():
            pltpu.make_async_copy(src, dst, a_recv).start()

        @pl.when(jnp.logical_not(is_home))
        def _():
            remote(src, dst, a_send, a_recv, device).start()

    @pl.loop(1, NC)
    def _(j):
        for src, dst, device in send_a(j):
            remote(src, dst, a_send, a_recv, device).start()

    @pl.loop(0, NR)
    def _(i):
        start = i * rows
        pltpu.make_async_copy(
            l_hbm.at[pl.ds(start, rows)], lst.at[pl.ds(start, rows)], l_sem.at[i]
        ).wait()
        for k in range(NSUP):
            mask = structure[k, pr * NR + i].astype(F32)
            for col in range(S // 128):
                v = lst[pl.ds(start + col * NSUP + k, BLK, stride=S * NSUP // 128), :] * mask
                hi, lo = split(v)
                xhi[k, pl.ds(i * BLK, BLK), pl.ds(col * 128, 128)] = hi
                xlo[k, pl.ds(i * BLK, BLK), pl.ds(col * 128, 128)] = lo

    await_bytes(abuf, a_recv)
    hi, lo = split(abuf[...])
    ahi[...] = hi
    alo[...] = lo

    def z_copies(j):
        cols = pl.ds(pl.multiple_of(j * W, W), W)
        return [
            remote(ybuf.at[pl.ds(h * 64, 64), cols], zr.at[h, :, cols], z_send, z_recv.at[h, j], device)
            for h, device in enumerate((z_down, z_up))
        ]

    @pl.loop(0, NCH)
    def _(j):
        cols = pl.ds(pl.multiple_of(j * W, W), W)
        k = div(j, PER_K)
        kcols = pl.ds(pl.multiple_of(rem(j, PER_K) * W, W), W)
        ybuf[:, cols] = dot3(ahi[...], alo[...], xhi[k, :, kcols], xlo[k, :, kcols])
        for copy in z_copies(j):
            copy.start()

    def x_stage(buf, row0, far, final, far_send, far_recv, final_send, final_recv):
        def first(j):
            cols = pl.ds(pl.multiple_of(j * W, W), W)
            return [
                remote(
                    buf.at[pl.ds(pl.multiple_of(row0 + x_far * 32 + h * 16, 16), 16), cols],
                    far.at[h, :, cols], far_send, far_recv.at[h, j], device,
                )
                for h, device in enumerate((right, left))
            ]

        def second(j):
            cols = pl.ds(pl.multiple_of(j * W, W), W)
            return [
                remote(
                    buf.at[pl.ds(pl.multiple_of(row0 + target * 32, 32), 32), cols],
                    final.at[h, :, cols], final_send, final_recv.at[h, j], device,
                )
                for h, (device, target) in enumerate(((right, x_next), (left, x_prev)))
            ]

        def send_first(j):
            for copy in first(j):
                copy.start()

        def send_second(j):
            cols = pl.ds(pl.multiple_of(j * W, W), W)
            for h, (copy, target) in enumerate(zip(first(j), (x_next, x_prev))):
                copy.wait_recv()
                rows_h = pl.ds(pl.multiple_of(row0 + target * 32 + h * 16, 16), 16)
                buf[rows_h, cols] += far[h, :, cols]
            for copy in second(j):
                copy.start()

        def total(j):
            cols = pl.ds(pl.multiple_of(j * W, W), W)
            for copy in second(j):
                copy.wait_recv()
            mine = pl.ds(pl.multiple_of(row0 + x * 32, 32), 32)
            return buf[mine, cols] + (final[0, :, cols] + final[1, :, cols])

        return send_first, send_second, total

    y_first, y_second, y_total = x_stage(ybuf, 128, xo, xf, xo_send, xo_recv, xf_send, xf_recv)
    d_first, d_second, d_total = x_stage(dbuf, 0, dxo, dxf, dxo_send, dxo_recv, dxf_send, dxf_recv)

    def add_z(j):
        cols = pl.ds(pl.multiple_of(j * W, W), W)
        for h, copy in enumerate(z_copies(j)):
            copy.wait_recv()
            for target in range(NX):
                ybuf[pl.ds(128 + target * 32 + h * 16, 16), cols] += zr[h, pl.ds(target * 16, 16), cols]
        y_first(j)

    def finish_c(j):
        cols = pl.ds(pl.multiple_of(j * W, W), W)
        k = div(j, PER_K)
        mask = structure[k, pr * NR + home].astype(F32)
        out_c[:, cols] = -mask * y_total(j)
        for i in range(W // T):
            q = rem(j, PER_K) * (W // T) + i
            src = out_c.at[:, pl.ds(pl.multiple_of(j * W + i * T, T), T)]
            dst = cbuf.at[k, pl.ds(pl.multiple_of(pc * 32, 32), 32)]

            @pl.when(q == pc)
            def _():
                pltpu.make_async_copy(src, dst, c_recv.at[k]).start()

            @pl.when(q != pc)
            def _():
                remote(src, dst, c_send, c_recv.at[k], (pr, q)).start()

    def second_product(k):
        await_bytes(cbuf.at[k], c_recv.at[k])
        chi, clo = split(cbuf[k].T)

        @pl.loop(0, PER_K)
        def _(n):
            j = k * PER_K + n
            cols = pl.ds(pl.multiple_of(j * W, W), W)
            kcols = pl.ds(pl.multiple_of(n * W, W), W)
            dbuf[:, cols] = dot3(chi, clo, xhi[k, :, kcols], xlo[k, :, kcols])
            d_first(j)

    def finish_d(j):
        cols = pl.ds(pl.multiple_of(j * W, W), W)
        k = div(j, PER_K)
        dsum[:, cols] = d_total(j)
        for i in range(W // T):
            q = rem(j, PER_K) * (W // T) + i
            src = dsum.at[:, pl.ds(pl.multiple_of(j * W + i * T, T), T)]
            dst = dfin.at[k, zl, pl.ds(pl.multiple_of(side * 128 + x * 32, 32), 32)]
            own = jnp.logical_and(is_home, q == pc)

            @pl.when(own)
            def _():
                pltpu.make_async_copy(src, dst, d_recv.at[k]).start()

            @pl.when(jnp.logical_not(own))
            def _():
                remote(src, dst, d_send, d_recv.at[k], (home, q)).start()

    @pl.loop(0, NCH)
    def _(j):
        add_z(j)

        @pl.when(j >= 1)
        def _():
            y_second(j - 1)

        @pl.when(j >= 2)
        def _():
            finish_c(j - 2)

    y_second(NCH - 1)
    second_product(0)
    finish_c(NCH - 2)
    finish_c(NCH - 1)

    @pl.loop(0, PER_K)
    def _(j):
        d_second(j)

    second_product(1)

    @pl.loop(0, PER_K)
    def _(j):
        finish_d(j)

    @pl.loop(PER_K, NCH)
    def _(j):
        d_second(j)

    @pl.loop(PER_K, NCH)
    def _(j):
        finish_d(j)

    for k in range(NSUP):
        await_bytes(dfin.at[k], d_recv.at[k])
        out_d[k] = piv[k] - (dfin[k, 0] + dfin[k, 1]).T

    await_bytes(abuf.at[pl.ds(0, 240)], a_send)

    @pl.when(jnp.logical_not(is_home))
    def _():
        await_bytes(abuf.at[pl.ds(0, 16)], a_send)

    await_bytes(zr, z_send)
    await_bytes(xo, xo_send)
    await_bytes(xf, xf_send)
    await_bytes(dxo, dxo_send)
    await_bytes(dxf, dxf_send)
    await_bytes(cbuf.at[:, pl.ds(0, 480)], c_send)
    await_bytes(dfin.at[:, :, pl.ds(0, 240)], d_send)

    @pl.when(jnp.logical_not(is_home))
    def _():
        await_bytes(dfin.at[:, :, pl.ds(0, 16)], d_send)


def body(ancestor_inverse, lower_panel, pivot_inverse, structure):
    part = lower_panel.shape[0]
    panel = lower_panel.reshape(part, NSUP, S // 128, 128).transpose(0, 2, 1, 3)
    panel = panel.reshape(part * NSUP * S // 128, 128)
    width = NSUP * S
    vmem = pl.BlockSpec(memory_space=pltpu.VMEM)
    hbm = pl.BlockSpec(memory_space=pl.ANY)
    dma = pltpu.SemaphoreType.DMA
    columns, diagonal = pl.pallas_call(
        kernel,
        name="selinv",
        out_shape=(
            jax.ShapeDtypeStruct((32, width), F32),
            jax.ShapeDtypeStruct(pivot_inverse.shape, F32),
        ),
        in_specs=[hbm, hbm, vmem, pl.BlockSpec(memory_space=pltpu.SMEM)],
        out_specs=(vmem, vmem),
        scratch_shapes=[
            pltpu.VMEM(panel.shape, F32),
            pltpu.VMEM((NSUP, part, S), BF16),
            pltpu.VMEM((NSUP, part, S), BF16),
            pltpu.VMEM((256, part), F32),
            pltpu.VMEM((256, part), BF16),
            pltpu.VMEM((256, part), BF16),
            pltpu.VMEM((256, width), F32),
            pltpu.VMEM((2, 64, width), F32),
            pltpu.VMEM((2, 16, width), F32),
            pltpu.VMEM((2, 32, width), F32),
            pltpu.VMEM((NSUP, part, T), F32),
            pltpu.VMEM((128, width), F32),
            pltpu.VMEM((2, 16, width), F32),
            pltpu.VMEM((2, 32, width), F32),
            pltpu.VMEM((32, width), F32),
            pltpu.VMEM((NSUP, 2, 256, 128), F32),
            dma((NR,)),
            dma(()),
            dma(()),
            dma(()),
            dma((2, NCH)),
            dma(()),
            dma((2, NCH)),
            dma(()),
            dma((2, NCH)),
            dma(()),
            dma((NSUP,)),
            dma(()),
            dma((2, NCH)),
            dma(()),
            dma((2, NCH)),
            dma(()),
            dma((NSUP,)),
        ],
        compiler_params=pltpu.CompilerParams(
            collective_id=0, has_side_effects=True, vmem_limit_bytes=60 * 2**20
        ),
    )(ancestor_inverse, panel, pivot_inverse, structure)
    return columns.reshape(32, NSUP, S), diagonal


def solution(mesh):
    return jax.shard_map(
        body,
        mesh=mesh,
        in_specs=(P("prow", "pcol"), P("prow", None, None), P(None, "pcol", "prow"), P()),
        out_specs=(P(("prow", "pcol"), None, None), P(None, "pcol", "prow")),
        check_vma=False,
    )
```

```python
import functools

import jax
import jax.numpy as jnp
from jax import lax
from jax.experimental import pallas as pl
from jax.experimental.pallas import tpu as pltpu
from jax.sharding import PartitionSpec as P

MESH = pl.DeviceIdType.MESH
F32 = jnp.float32
BF16 = jnp.bfloat16
S = 2048
NSUP = 2
BLK = 64
NX, NY, NZ = 4, 4, 4
NR, NC = 8, 16
W = 512
NCH = NSUP * S // W
PER_K = S // W
T = S // NC


def split(v):
    hi = v.astype(BF16)
    return hi, (v - hi.astype(F32)).astype(BF16)


def dot3(ahi, alo, bhi, blo):
    dot = functools.partial(jnp.dot, preferred_element_type=F32)
    return dot(ahi, bhi) + (dot(ahi, blo) + dot(alo, bhi))


def kernel(
    a_hbm, l_hbm, piv, structure, out_c, out_d,
    lst, xhi, xlo, mid, abuf, ahi, alo, ybuf, zr, xo, xf, cbuf, dbuf, dxo, dxf, dsum, dfin,
    l_sem, m_send, m_recv, a_send, a_recv, z_send, z_recv, xo_send, xo_recv, xf_send, xf_recv,
    c_send, c_recv, dxo_send, dxo_recv, dxf_send, dxf_recv, d_send, d_recv,
):
    pr, pc = lax.axis_index("prow"), lax.axis_index("pcol")
    rem, div = lax.rem, lax.div
    x, zl = div(pr, 2), rem(pr, 2)
    zh, rest = div(pc, 8), rem(pc, 8)
    z = 2 * zh + zl
    y, core = div(rest, 2), rem(pc, 2)

    def at_z(zz):
        return (x * 2 + rem(zz, 2), div(zz, 2) * 8 + rest)

    def at_xz(xx, zz):
        return (xx * 2 + rem(zz, 2), div(zz, 2) * 8 + rest)

    def at_x(xx):
        return (xx * 2 + zl, pc)

    z_down, z_up = at_z(rem(z + 3, 4)), at_z(rem(z + 1, 4))
    x_next, x_prev, x_far = rem(x + 1, 4), rem(x + 3, 4), rem(x + 2, 4)
    right, left = at_x(x_next), at_x(x_prev)

    def remote(src, dst, send, recv, device):
        return pltpu.make_async_remote_copy(
            src_ref=src, dst_ref=dst, send_sem=send, recv_sem=recv,
            device_id=device, device_id_type=MESH,
        )

    def await_bytes(ref, sem):
        pltpu.make_async_copy(ref, ref, sem).wait()

    rows = S * NSUP * BLK // 128
    l_copies = [
        pltpu.make_async_copy(
            l_hbm.at[pl.ds(i * rows, rows)], lst.at[pl.ds(i * rows, rows)], l_sem.at[i]
        )
        for i in range(NR)
    ]
    for copy in l_copies:
        copy.start()

    barrier = pltpu.get_barrier_semaphore()

    def greet(device):
        pl.semaphore_signal(barrier, inc=1, device_id=device, device_id_type=MESH)

    for j in range(1, NC):
        greet((pr, rem(pc + j, NC)))
    for j in range(NX):
        xx = rem(x + j, NX)
        if j:
            greet(at_xz(xx, z))
        greet(at_xz(xx, rem(z + 1, NZ)))
        greet(at_xz(xx, rem(z + 3, NZ)))

    def prepare(i):
        start = i * rows
        pltpu.make_async_copy(
            l_hbm.at[pl.ds(start, rows)], lst.at[pl.ds(start, rows)], l_sem.at[i]
        ).wait()
        for k in range(NSUP):
            mask = structure[k, pr * NR + i].astype(F32)
            for col in range(S // 128):
                v = lst[pl.ds(start + col * NSUP + k, BLK, stride=S * NSUP // 128), :] * mask
                hi, lo = split(v)
                xhi[k, pl.ds(i * BLK, BLK), pl.ds(col * 128, 128)] = hi
                xlo[k, pl.ds(i * BLK, BLK), pl.ds(col * 128, 128)] = lo

    pl.semaphore_wait(barrier, NC - 1 + 3 * NX - 1)

    def a_piece(q):
        src = a_hbm.at[pl.ds(pl.multiple_of(q * 32, 32), 32)]
        dst = mid.at[:, pl.ds(pl.multiple_of(pc * 256, 256), 256)]
        return src, dst

    pltpu.make_async_copy(*a_piece(pc), m_recv.at[div(pc, 2)]).start()

    @pl.loop(1, NC)
    def _(j):
        q = rem(pc + j, NC)
        src, dst = a_piece(q)
        remote(src, dst, m_send, m_recv.at[div(pc, 2)], (pr, q)).start()

    def forward(target, moved):
        xx = rem(x + target, NX)
        tl = 1 - zl if moved else zl
        column = xx * 2 + tl
        cols = pl.ds(pl.multiple_of(column * 512, 512), 512)
        await_bytes(mid.at[:, cols], m_recv.at[column])
        if moved:
            for h in range(2):
                remote(
                    mid.at[pl.ds(h * 16, 16), cols],
                    abuf.at[pl.ds(pl.multiple_of(h * 64 + x * 16, 16), 16)],
                    a_send, a_recv.at[0], at_xz(xx, rem(z + (1 if h == 0 else 3), NZ)),
                ).start()
        else:
            dst = abuf.at[pl.ds(pl.multiple_of(128 + x * 32, 32), 32)]
            if target:
                remote(mid.at[:, cols], dst, a_send, a_recv.at[1], at_xz(xx, z)).start()
            else:
                pltpu.make_async_copy(mid.at[:, cols], dst, a_recv.at[1]).start()

    @pl.loop(0, 5)
    def _(i):
        prepare(i)

    for target in range(NX):
        forward(target, True)

    for target in range(NX):
        forward(target, False)

    @pl.loop(5, NR)
    def _(i):
        prepare(i)

    def z_copies(j):
        cols = pl.ds(pl.multiple_of(j * W, W), W)
        return [
            remote(ybuf.at[pl.ds(h * 64, 64), cols], zr.at[h, :, cols], z_send, z_recv.at[h, j], device)
            for h, device in enumerate((z_down, z_up))
        ]

    def first_product(g):
        part = pl.ds(g * 128, 128)
        await_bytes(abuf.at[part], a_recv.at[g])
        hi, lo = split(abuf[part])
        ahi[...] = hi
        alo[...] = lo

        @pl.loop(0, NCH)
        def _(j):
            cols = pl.ds(pl.multiple_of(j * W, W), W)
            k = div(j, PER_K)
            kcols = pl.ds(pl.multiple_of(rem(j, PER_K) * W, W), W)
            ybuf[part, cols] = dot3(ahi[...], alo[...], xhi[k, :, kcols], xlo[k, :, kcols])
            if g == 0:
                for copy in z_copies(j):
                    copy.start()

    first_product(0)
    first_product(1)

    def x_stage(buf, row0, far, final, far_send, far_recv, final_send, final_recv):
        def first(j):
            cols = pl.ds(pl.multiple_of(j * W, W), W)
            return [
                remote(
                    buf.at[pl.ds(pl.multiple_of(row0 + x_far * 32 + h * 16, 16), 16), cols],
                    far.at[h, :, cols], far_send, far_recv.at[h, j], device,
                )
                for h, device in enumerate((right, left))
            ]

        def second(j):
            cols = pl.ds(pl.multiple_of(j * W, W), W)
            return [
                remote(
                    buf.at[pl.ds(pl.multiple_of(row0 + target * 32, 32), 32), cols],
                    final.at[h, :, cols], final_send, final_recv.at[h, j], device,
                )
                for h, (device, target) in enumerate(((right, x_next), (left, x_prev)))
            ]

        def send_first(j):
            for copy in first(j):
                copy.start()

        def send_second(j):
            cols = pl.ds(pl.multiple_of(j * W, W), W)
            for h, (copy, target) in enumerate(zip(first(j), (x_next, x_prev))):
                copy.wait_recv()
                rows_h = pl.ds(pl.multiple_of(row0 + target * 32 + h * 16, 16), 16)
                buf[rows_h, cols] += far[h, :, cols]
            for copy in second(j):
                copy.start()

        def total(j):
            cols = pl.ds(pl.multiple_of(j * W, W), W)
            for copy in second(j):
                copy.wait_recv()
            mine = pl.ds(pl.multiple_of(row0 + x * 32, 32), 32)
            return buf[mine, cols] + (final[0, :, cols] + final[1, :, cols])

        return send_first, send_second, total

    y_first, y_second, y_total = x_stage(ybuf, 128, xo, xf, xo_send, xo_recv, xf_send, xf_recv)
    d_first, d_second, d_total = x_stage(dbuf, 0, dxo, dxf, dxo_send, dxo_recv, dxf_send, dxf_recv)

    def add_z(j):
        cols = pl.ds(pl.multiple_of(j * W, W), W)
        for h, copy in enumerate(z_copies(j)):
            copy.wait_recv()
            for target in range(NX):
                ybuf[pl.ds(128 + target * 32 + h * 16, 16), cols] += zr[h, pl.ds(target * 16, 16), cols]
        y_first(j)

    def finish_c(j):
        cols = pl.ds(pl.multiple_of(j * W, W), W)
        k = div(j, PER_K)
        mask = structure[k, pr * NR + div(pc, 2)].astype(F32)
        out_c[:, cols] = -mask * y_total(j)
        for i in range(W // T):
            tx = rem(j, PER_K)
            q = (i // 2) * 8 + ((i % 2) * 2 + rem(tx + k, 2)) * 2 + div(tx, 2)
            src = out_c.at[:, pl.ds(pl.multiple_of(j * W + i * T, T), T)]
            dst = cbuf.at[k, pl.ds(pl.multiple_of(pc * 32, 32), 32)]

            @pl.when(q == pc)
            def _():
                pltpu.make_async_copy(src, dst, c_recv.at[k]).start()

            @pl.when(q != pc)
            def _():
                remote(src, dst, c_send, c_recv.at[k], (pr, q)).start()

    def second_product(k):
        await_bytes(cbuf.at[k], c_recv.at[k])
        chi, clo = split(cbuf[k].T)

        @pl.loop(0, PER_K)
        def _(n):
            j = k * PER_K + n
            cols = pl.ds(pl.multiple_of(j * W, W), W)
            kcols = pl.ds(pl.multiple_of(n * W, W), W)
            dbuf[:, cols] = dot3(chi, clo, xhi[k, :, kcols], xlo[k, :, kcols])
            d_first(j)

    def finish_d(j):
        cols = pl.ds(pl.multiple_of(j * W, W), W)
        k = div(j, PER_K)
        dsum[:, cols] = d_total(j)
        for i in range(W // T):
            q = rem(j, PER_K) * (W // T) + i
            src = dsum.at[:, pl.ds(pl.multiple_of(j * W + i * T, T), T)]
            dst = dfin.at[k, zl, pl.ds(pl.multiple_of(div(y, 2) * 128 + x * 32, 32), 32)]
            owner = (2 * core + rem(y + k, 2)) * 2 + zh
            own = jnp.logical_and(owner == pr, q == pc)

            @pl.when(own)
            def _():
                pltpu.make_async_copy(src, dst, d_recv.at[k]).start()

            @pl.when(jnp.logical_not(own))
            def _():
                remote(src, dst, d_send, d_recv.at[k], (owner, q)).start()

    def y_step(j):
        add_z(j)

        @pl.when(j >= 1)
        def _():
            y_second(j - 1)

        @pl.when(j >= 2)
        def _():
            finish_c(j - 2)

    @pl.loop(0, NCH - 1)
    def _(j):
        y_step(j)

    second_product(0)
    add_z(NCH - 1)
    y_second(NCH - 2)
    finish_c(NCH - 3)

    @pl.loop(0, PER_K)
    def _(j):
        d_second(j)

    y_second(NCH - 1)
    finish_c(NCH - 2)

    @pl.loop(0, PER_K)
    def _(j):
        finish_d(j)

    finish_c(NCH - 1)
    second_product(1)

    @pl.loop(PER_K, NCH)
    def _(j):
        d_second(j)

    @pl.loop(PER_K, NCH)
    def _(j):
        finish_d(j)

    for k in range(NSUP):
        await_bytes(dfin.at[k], d_recv.at[k])
        out_d[k] = piv[k] - (dfin[k, 0] + dfin[k, 1]).T

    await_bytes(abuf.at[pl.ds(0, 240)], m_send)
    await_bytes(abuf.at[pl.ds(0, 224)], a_send)
    await_bytes(zr, z_send)
    await_bytes(xo, xo_send)
    await_bytes(xf, xf_send)
    await_bytes(dxo, dxo_send)
    await_bytes(dxf, dxf_send)
    await_bytes(cbuf.at[:, pl.ds(0, 480)], c_send)
    await_bytes(abuf.at[pl.ds(0, 248)], d_send)

    @pl.when(jnp.logical_not(jnp.logical_and(zh == zl, div(x, 2) == core)))
    def _():
        await_bytes(abuf.at[pl.ds(0, 8)], d_send)


def body(ancestor_inverse, lower_panel, pivot_inverse, structure):
    part = lower_panel.shape[0]
    panel = lower_panel.reshape(part, NSUP, S // 128, 128).transpose(0, 2, 1, 3)
    panel = panel.reshape(part * NSUP * S // 128, 128)
    width = NSUP * S
    vmem = pl.BlockSpec(memory_space=pltpu.VMEM)
    hbm = pl.BlockSpec(memory_space=pl.ANY)
    dma = pltpu.SemaphoreType.DMA
    columns, diagonal = pl.pallas_call(
        kernel,
        name="selinv",
        out_shape=(
            jax.ShapeDtypeStruct((32, width), F32),
            jax.ShapeDtypeStruct(pivot_inverse.shape, F32),
        ),
        in_specs=[hbm, hbm, vmem, pl.BlockSpec(memory_space=pltpu.SMEM)],
        out_specs=(vmem, vmem),
        scratch_shapes=[
            pltpu.VMEM(panel.shape, F32),
            pltpu.VMEM((NSUP, part, S), BF16),
            pltpu.VMEM((NSUP, part, S), BF16),
            pltpu.VMEM((32, NR * part), F32),
            pltpu.VMEM((256, part), F32),
            pltpu.VMEM((128, part), BF16),
            pltpu.VMEM((128, part), BF16),
            pltpu.VMEM((256, width), F32),
            pltpu.VMEM((2, 64, width), F32),
            pltpu.VMEM((2, 16, width), F32),
            pltpu.VMEM((2, 32, width), F32),
            pltpu.VMEM((NSUP, part, T), F32),
            pltpu.VMEM((128, width), F32),
            pltpu.VMEM((2, 16, width), F32),
            pltpu.VMEM((2, 32, width), F32),
            pltpu.VMEM((32, width), F32),
            pltpu.VMEM((NSUP, 2, 256, 128), F32),
            dma((NR,)),
            dma(()),
            dma((NR,)),
            dma(()),
            dma((2,)),
            dma(()),
            dma((2, NCH)),
            dma(()),
            dma((2, NCH)),
            dma(()),
            dma((2, NCH)),
            dma(()),
            dma((NSUP,)),
            dma(()),
            dma((2, NCH)),
            dma(()),
            dma((2, NCH)),
            dma(()),
            dma((NSUP,)),
        ],
        compiler_params=pltpu.CompilerParams(
            collective_id=0, has_side_effects=True, vmem_limit_bytes=60 * 2**20
        ),
    )(ancestor_inverse, panel, pivot_inverse, structure)
    return columns.reshape(32, NSUP, S), diagonal


def solution(mesh):
    return jax.shard_map(
        body,
        mesh=mesh,
        in_specs=(P("prow", "pcol"), P("prow", None, None), P(None, "pcol", "prow"), P()),
        out_specs=(P(("prow", "pcol"), None, None), P(None, "pcol", "prow")),
        check_vma=False,
    )
```

```python
import functools

import jax
import jax.numpy as jnp
from jax import lax
from jax.experimental import pallas as pl
from jax.experimental.pallas import tpu as pltpu
from jax.sharding import PartitionSpec as P

MESH = pl.DeviceIdType.MESH
F32 = jnp.float32
BF16 = jnp.bfloat16
S = 2048
NSUP = 2
BLK = 64
NX, NY, NZ = 4, 4, 4
NR, NC = 8, 16
W = 512
NCH = NSUP * S // W
PER_K = S // W
T = S // NC


def split(v):
    hi = v.astype(BF16)
    return hi, (v - hi.astype(F32)).astype(BF16)


def dot3(ahi, alo, bhi, blo):
    dot = functools.partial(jnp.dot, preferred_element_type=F32)
    return dot(ahi, bhi) + (dot(ahi, blo) + dot(alo, bhi))


def kernel(
    a_hbm, l_hbm, piv_hbm, structure_hbm, out_c, out_d,
    piv, structure, lst, xhi, xlo, mid, abuf, ahi, alo, ybuf, zr, xo, xf, cbuf, dbuf, dxo, dxf, dsum, dfin,
    piv_sem, structure_sem, l_sem, m_send, m_recv, a_send, a_recv, z_send, z_recv, xo_send, xo_recv, xf_send, xf_recv,
    c_send, c_recv, dxo_send, dxo_recv, dxf_send, dxf_recv, d_send, d_recv,
):
    pr, pc = lax.axis_index("prow"), lax.axis_index("pcol")
    rem, div = lax.rem, lax.div
    x, zl = div(pr, 2), rem(pr, 2)
    zh, rest = div(pc, 8), rem(pc, 8)
    z = 2 * zh + zl
    y, core = div(rest, 2), rem(pc, 2)

    def at_z(zz):
        return (x * 2 + rem(zz, 2), div(zz, 2) * 8 + rest)

    def at_xz(xx, zz):
        return (xx * 2 + rem(zz, 2), div(zz, 2) * 8 + rest)

    def at_x(xx):
        return (xx * 2 + zl, pc)

    z_down, z_up = at_z(rem(z + 3, 4)), at_z(rem(z + 1, 4))
    x_next, x_prev, x_far = rem(x + 1, 4), rem(x + 3, 4), rem(x + 2, 4)
    right, left = at_x(x_next), at_x(x_prev)

    def remote(src, dst, send, recv, device):
        return pltpu.make_async_remote_copy(
            src_ref=src, dst_ref=dst, send_sem=send, recv_sem=recv,
            device_id=device, device_id_type=MESH,
        )

    def await_bytes(ref, sem):
        pltpu.make_async_copy(ref, ref, sem).wait()

    rows = S * NSUP * BLK // 128
    l_copies = [
        pltpu.make_async_copy(
            l_hbm.at[pl.ds(i * rows, rows)], lst.at[pl.ds(i * rows, rows)], l_sem.at[i]
        )
        for i in range(NR)
    ]
    structure_copy = pltpu.make_async_copy(structure_hbm, structure, structure_sem)
    structure_copy.start()
    for copy in l_copies:
        copy.start()
    piv_copy = pltpu.make_async_copy(piv_hbm, piv, piv_sem)
    piv_copy.start()

    barrier = pltpu.get_barrier_semaphore()

    def greet(device):
        pl.semaphore_signal(barrier, inc=1, device_id=device, device_id_type=MESH)

    for j in range(1, NC):
        greet((pr, rem(pc + j, NC)))
    for j in range(NX):
        xx = rem(x + j, NX)
        if j:
            greet(at_xz(xx, z))
        greet(at_xz(xx, rem(z + 1, NZ)))
        greet(at_xz(xx, rem(z + 3, NZ)))

    def prepare(i):
        start = i * rows
        pltpu.make_async_copy(
            l_hbm.at[pl.ds(start, rows)], lst.at[pl.ds(start, rows)], l_sem.at[i]
        ).wait()
        for k in range(NSUP):
            mask = structure[k, pr * NR + i].astype(F32)
            for col in range(S // 128):
                v = lst[pl.ds(start + col * NSUP + k, BLK, stride=S * NSUP // 128), :] * mask
                hi, lo = split(v)
                xhi[k, pl.ds(i * BLK, BLK), pl.ds(col * 128, 128)] = hi
                xlo[k, pl.ds(i * BLK, BLK), pl.ds(col * 128, 128)] = lo

    pl.semaphore_wait(barrier, NC - 1 + 3 * NX - 1)

    def a_piece(q):
        src = a_hbm.at[pl.ds(pl.multiple_of(q * 32, 32), 32)]
        dst = mid.at[:, pl.ds(pl.multiple_of(pc * 256, 256), 256)]
        return src, dst

    pltpu.make_async_copy(*a_piece(pc), m_recv.at[div(pc, 2)]).start()

    @pl.loop(1, NC)
    def _(j):
        q = rem(pc + j, NC)
        src, dst = a_piece(q)
        remote(src, dst, m_send, m_recv.at[div(pc, 2)], (pr, q)).start()

    def forward(target, moved):
        xx = rem(x + target, NX)
        tl = 1 - zl if moved else zl
        column = xx * 2 + tl
        cols = pl.ds(pl.multiple_of(column * 512, 512), 512)
        await_bytes(mid.at[:, cols], m_recv.at[column])
        if moved:
            for h in range(2):
                remote(
                    mid.at[pl.ds(h * 16, 16), cols],
                    abuf.at[pl.ds(pl.multiple_of(h * 64 + x * 16, 16), 16)],
                    a_send, a_recv.at[0], at_xz(xx, rem(z + (1 if h == 0 else 3), NZ)),
                ).start()
        else:
            dst = abuf.at[pl.ds(pl.multiple_of(128 + x * 32, 32), 32)]
            if target:
                remote(mid.at[:, cols], dst, a_send, a_recv.at[1], at_xz(xx, z)).start()
            else:
                pltpu.make_async_copy(mid.at[:, cols], dst, a_recv.at[1]).start()

    structure_copy.wait()

    @pl.loop(0, 5)
    def _(i):
        prepare(i)

    for target in range(NX):
        forward(target, True)

    for target in range(NX):
        forward(target, False)

    @pl.loop(5, NR)
    def _(i):
        prepare(i)

    def z_copies(j):
        cols = pl.ds(pl.multiple_of(j * W, W), W)
        return [
            remote(ybuf.at[pl.ds(h * 64, 64), cols], zr.at[h, :, cols], z_send, z_recv.at[h, j], device)
            for h, device in enumerate((z_down, z_up))
        ]

    def first_product(g):
        part = pl.ds(g * 128, 128)
        await_bytes(abuf.at[part], a_recv.at[g])
        hi, lo = split(abuf[part])
        ahi[...] = hi
        alo[...] = lo

        @pl.loop(0, NCH)
        def _(j):
            cols = pl.ds(pl.multiple_of(j * W, W), W)
            k = div(j, PER_K)
            kcols = pl.ds(pl.multiple_of(rem(j, PER_K) * W, W), W)
            ybuf[part, cols] = dot3(ahi[...], alo[...], xhi[k, :, kcols], xlo[k, :, kcols])
            if g == 0:
                for copy in z_copies(j):
                    copy.start()

    first_product(0)
    first_product(1)

    def x_stage(buf, row0, far, final, far_send, far_recv, final_send, final_recv):
        def first(j):
            cols = pl.ds(pl.multiple_of(j * W, W), W)
            return [
                remote(
                    buf.at[pl.ds(pl.multiple_of(row0 + x_far * 32 + h * 16, 16), 16), cols],
                    far.at[h, :, cols], far_send, far_recv.at[h, j], device,
                )
                for h, device in enumerate((right, left))
            ]

        def second(j):
            cols = pl.ds(pl.multiple_of(j * W, W), W)
            return [
                remote(
                    buf.at[pl.ds(pl.multiple_of(row0 + target * 32, 32), 32), cols],
                    final.at[h, :, cols], final_send, final_recv.at[h, j], device,
                )
                for h, (device, target) in enumerate(((right, x_next), (left, x_prev)))
            ]

        def send_first(j):
            for copy in first(j):
                copy.start()

        def send_second(j):
            cols = pl.ds(pl.multiple_of(j * W, W), W)
            for h, (copy, target) in enumerate(zip(first(j), (x_next, x_prev))):
                copy.wait_recv()
                rows_h = pl.ds(pl.multiple_of(row0 + target * 32 + h * 16, 16), 16)
                buf[rows_h, cols] += far[h, :, cols]
            for copy in second(j):
                copy.start()

        def total(j):
            cols = pl.ds(pl.multiple_of(j * W, W), W)
            for copy in second(j):
                copy.wait_recv()
            mine = pl.ds(pl.multiple_of(row0 + x * 32, 32), 32)
            return buf[mine, cols] + (final[0, :, cols] + final[1, :, cols])

        return send_first, send_second, total

    y_first, y_second, y_total = x_stage(ybuf, 128, xo, xf, xo_send, xo_recv, xf_send, xf_recv)
    d_first, d_second, d_total = x_stage(dbuf, 0, dxo, dxf, dxo_send, dxo_recv, dxf_send, dxf_recv)

    def add_z(j):
        cols = pl.ds(pl.multiple_of(j * W, W), W)
        for h, copy in enumerate(z_copies(j)):
            copy.wait_recv()
            for target in range(NX):
                ybuf[pl.ds(128 + target * 32 + h * 16, 16), cols] += zr[h, pl.ds(target * 16, 16), cols]
        y_first(j)

    def finish_c(j):
        cols = pl.ds(pl.multiple_of(j * W, W), W)
        k = div(j, PER_K)
        mask = structure[k, pr * NR + div(pc, 2)].astype(F32)
        out_c[:, cols] = -mask * y_total(j)
        for i in range(W // T):
            tx = rem(j, PER_K)
            q = (i // 2) * 8 + ((i % 2) * 2 + rem(tx + k, 2)) * 2 + div(tx, 2)
            src = out_c.at[:, pl.ds(pl.multiple_of(j * W + i * T, T), T)]
            dst = cbuf.at[k, pl.ds(pl.multiple_of(pc * 32, 32), 32)]

            @pl.when(q == pc)
            def _():
                pltpu.make_async_copy(src, dst, c_recv.at[k]).start()

            @pl.when(q != pc)
            def _():
                remote(src, dst, c_send, c_recv.at[k], (pr, q)).start()

    def second_product(k):
        await_bytes(cbuf.at[k], c_recv.at[k])
        chi, clo = split(cbuf[k].T)

        @pl.loop(0, PER_K)
        def _(n):
            j = k * PER_K + n
            cols = pl.ds(pl.multiple_of(j * W, W), W)
            kcols = pl.ds(pl.multiple_of(n * W, W), W)
            dbuf[:, cols] = dot3(chi, clo, xhi[k, :, kcols], xlo[k, :, kcols])
            d_first(j)

    def finish_d(j):
        cols = pl.ds(pl.multiple_of(j * W, W), W)
        k = div(j, PER_K)
        dsum[:, cols] = d_total(j)
        for i in range(W // T):
            q = rem(j, PER_K) * (W // T) + i
            src = dsum.at[:, pl.ds(pl.multiple_of(j * W + i * T, T), T)]
            dst = dfin.at[k, zl, pl.ds(pl.multiple_of(div(y, 2) * 128 + x * 32, 32), 32)]
            owner = (2 * core + rem(y + k, 2)) * 2 + zh
            own = jnp.logical_and(owner == pr, q == pc)

            @pl.when(own)
            def _():
                pltpu.make_async_copy(src, dst, d_recv.at[k]).start()

            @pl.when(jnp.logical_not(own))
            def _():
                remote(src, dst, d_send, d_recv.at[k], (owner, q)).start()

    def y_step(j):
        add_z(j)

        @pl.when(j >= 1)
        def _():
            y_second(j - 1)

        @pl.when(j >= 2)
        def _():
            finish_c(j - 2)

    @pl.loop(0, NCH - 1)
    def _(j):
        y_step(j)

    y_step(NCH - 1)
    y_second(NCH - 1)
    second_product(0)
    finish_c(NCH - 2)
    finish_c(NCH - 1)

    @pl.loop(0, PER_K)
    def _(j):
        d_second(j)

    second_product(1)

    @pl.loop(0, PER_K)
    def _(j):
        d_second(PER_K + j)
        finish_d(j)

    @pl.loop(PER_K, NCH)
    def _(j):
        finish_d(j)

    piv_copy.wait()
    for k in range(NSUP):
        await_bytes(dfin.at[k], d_recv.at[k])
        out_d[k] = piv[k] - (dfin[k, 0] + dfin[k, 1]).T

    await_bytes(abuf.at[pl.ds(0, 240)], m_send)
    await_bytes(abuf.at[pl.ds(0, 224)], a_send)
    await_bytes(zr, z_send)
    await_bytes(xo, xo_send)
    await_bytes(xf, xf_send)
    await_bytes(dxo, dxo_send)
    await_bytes(dxf, dxf_send)
    await_bytes(cbuf.at[:, pl.ds(0, 480)], c_send)
    await_bytes(abuf.at[pl.ds(0, 248)], d_send)

    @pl.when(jnp.logical_not(jnp.logical_and(zh == zl, div(x, 2) == core)))
    def _():
        await_bytes(abuf.at[pl.ds(0, 8)], d_send)


def body(ancestor_inverse, lower_panel, pivot_inverse, structure):
    part = lower_panel.shape[0]
    panel = lower_panel.reshape(part, NSUP, S // 128, 128).transpose(0, 2, 1, 3)
    panel = panel.reshape(part * NSUP * S // 128, 128)
    width = NSUP * S
    vmem = pl.BlockSpec(memory_space=pltpu.VMEM)
    hbm = pl.BlockSpec(memory_space=pltpu.HBM)
    dma = pltpu.SemaphoreType.DMA
    columns, diagonal = pl.pallas_call(
        kernel,
        name="selinv",
        out_shape=(
            jax.ShapeDtypeStruct((32, width), F32),
            jax.ShapeDtypeStruct(pivot_inverse.shape, F32),
        ),
        in_specs=[hbm, hbm, hbm, hbm],
        out_specs=(vmem, vmem),
        scratch_shapes=[
            pltpu.VMEM(pivot_inverse.shape, F32),
            pltpu.SMEM(structure.shape, structure.dtype),
            pltpu.VMEM(panel.shape, F32),
            pltpu.VMEM((NSUP, part, S), BF16),
            pltpu.VMEM((NSUP, part, S), BF16),
            pltpu.VMEM((32, NR * part), F32),
            pltpu.VMEM((256, part), F32),
            pltpu.VMEM((128, part), BF16),
            pltpu.VMEM((128, part), BF16),
            pltpu.VMEM((256, width), F32),
            pltpu.VMEM((2, 64, width), F32),
            pltpu.VMEM((2, 16, width), F32),
            pltpu.VMEM((2, 32, width), F32),
            pltpu.VMEM((NSUP, part, T), F32),
            pltpu.VMEM((128, width), F32),
            pltpu.VMEM((2, 16, width), F32),
            pltpu.VMEM((2, 32, width), F32),
            pltpu.VMEM((32, width), F32),
            pltpu.VMEM((NSUP, 2, 256, 128), F32),
            dma(()),
            dma(()),
            dma((NR,)),
            dma(()),
            dma((NR,)),
            dma(()),
            dma((2,)),
            dma(()),
            dma((2, NCH)),
            dma(()),
            dma((2, NCH)),
            dma(()),
            dma((2, NCH)),
            dma(()),
            dma((NSUP,)),
            dma(()),
            dma((2, NCH)),
            dma(()),
            dma((2, NCH)),
            dma(()),
            dma((NSUP,)),
        ],
        compiler_params=pltpu.CompilerParams(
            collective_id=0, has_side_effects=True, vmem_limit_bytes=40 * 2**20
        ),
    )(
        *(
            pltpu.with_memory_space_constraint(v, pltpu.HBM)
            for v in (ancestor_inverse, panel, pivot_inverse, structure)
        )
    )
    return columns.reshape(32, NSUP, S), diagonal


def solution(mesh):
    return jax.shard_map(
        body,
        mesh=mesh,
        in_specs=(P("prow", "pcol"), P("prow", None, None), P(None, "pcol", "prow"), P()),
        out_specs=(P(("prow", "pcol"), None, None), P(None, "pcol", "prow")),
        check_vma=False,
    )
```

```python
import functools

import jax
import jax.numpy as jnp
from jax import lax
from jax.experimental import pallas as pl
from jax.experimental.pallas import tpu as pltpu
from jax.sharding import PartitionSpec as P

MESH = pl.DeviceIdType.MESH
F32 = jnp.float32
BF16 = jnp.bfloat16
S = 2048
NSUP = 2
BLK = 64
NX, NZ = 4, 4
NR, NC = 8, 16
PART = 512
DEPTH = 2 * PART
W = 512
NCH = S // W
ITEMS = 2 * NCH
EARLY = 4
LAG1, LAG2 = 2, 4
T = S // NC


def split(v):
    hi = v.astype(BF16)
    return hi, (v - hi.astype(F32)).astype(BF16)


def dot3(ahi, alo, bhi, blo):
    dot = functools.partial(jnp.dot, preferred_element_type=F32)
    return dot(ahi, bhi) + (dot(ahi, blo) + dot(alo, bhi))


def kernel(
    a_hbm, l_hbm, piv_hbm, structure_hbm, out_c, out_d,
    piv, structure, lst, xs, xin, xhi, xlo, mid, abuf, ahi, alo, ybuf, xo, xf,
    crow, cout, cbuf, dbuf, dxo, dxf, dsum, dfin,
    piv_sem, structure_sem, l_sem, m_send, m_recv, a_send, a_recv, n_send, n_recv,
    x_send, x_recv, p_send, p_recv, xo_send, xo_recv, xf_send, xf_recv,
    c_send, c_recv, o_send, o_recv, dxo_send, dxo_recv, dxf_send, dxf_recv, d_send, d_recv,
):
    rem, div = lax.rem, lax.div
    pr, pc = lax.axis_index("prow"), lax.axis_index("pcol")
    x, zl = div(pr, 2), rem(pr, 2)
    zh, rest = div(pc, 8), rem(pc, 8)
    y, core = div(rest, 2), rem(pc, 2)
    z = 2 * zh + zl
    other = 1 - zl

    def at_xz(xx, zz):
        return (xx * 2 + rem(zz, 2), div(zz, 2) * 8 + rest)

    z_down, z_up = at_xz(x, rem(z + 3, 4)), at_xz(x, rem(z + 1, 4))
    x_next, x_prev, x_far = rem(x + 1, 4), rem(x + 3, 4), rem(x + 2, 4)
    right, left = at_xz(x_next, z), at_xz(x_prev, z)
    partner = (pr, pc + 1 - 2 * core)

    def remote(src, dst, send, recv, device):
        return pltpu.make_async_remote_copy(
            src_ref=src, dst_ref=dst, send_sem=send, recv_sem=recv,
            device_id=device, device_id_type=MESH,
        )

    def await_bytes(ref, sem):
        pltpu.make_async_copy(ref, ref, sem).wait()

    def span(start, size):
        return pl.ds(pl.multiple_of(start, size), size)

    rows = BLK * NSUP * S // 128
    structure_copy = pltpu.make_async_copy(structure_hbm, structure, structure_sem)
    structure_copy.start()
    for i in range(NR):
        block = pl.ds(i * rows, rows)
        pltpu.make_async_copy(l_hbm.at[block], lst.at[block], l_sem.at[i]).start()
    piv_copy = pltpu.make_async_copy(piv_hbm, piv, piv_sem)
    piv_copy.start()

    barrier = pltpu.get_barrier_semaphore()

    def greet(device):
        pl.semaphore_signal(barrier, inc=1, device_id=device, device_id_type=MESH)

    for j in range(1, NC):
        greet((pr, rem(pc + j, NC)))
    for j in range(1, NX):
        greet(at_xz(rem(x + j, NX), z))
    greet(z_down)
    greet(z_up)
    pl.semaphore_wait(barrier, NC - 1 + NX - 1 + 2)

    def a_piece(q):
        src = a_hbm.at[span(q * 32, 32)]
        return src, mid.at[:, span(pc * 256, 256)], m_recv.at[div(pc, 4)]

    pltpu.make_async_copy(*a_piece(pc)).start()

    @pl.loop(1, NC)
    def _(j):
        q = rem(pc + j, NC)
        src, dst, recv = a_piece(q)
        remote(src, dst, m_send, recv, (pr, q)).start()

    structure_copy.wait()
    for i in range(NR):
        block = pl.ds(i * rows, rows)
        pltpu.make_async_copy(l_hbm.at[block], lst.at[block], l_sem.at[i]).wait()

    def pack(j):
        for part in range(2):
            for b in range(2):
                i = part * 4 + 2 * core + b
                mask = structure[other, pr * NR + i].astype(F32)
                for col in range(W // 128):
                    first = i * rows + (j * (W // 128) + col) * NSUP + other
                    v = lst[pl.ds(first, BLK, stride=S * NSUP // 128), :]
                    xs[pl.ds(part * 128 + b * BLK, BLK), span((j * (W // 128) + col) * 128, 128)] = v * mask

    def x_copies(j):
        cols = span(j * W, W)
        return [
            remote(
                xs.at[pl.ds(part * 128, 128), cols],
                xin.at[span(part * 256 + core * 128, 128), cols],
                x_send, x_recv.at[part, j], device,
            )
            for part, device in enumerate((z_up, z_down))
        ]

    def send_x(j):
        for copy in x_copies(j):
            copy.start()

    def p_copies(j):
        cols = span(j * W, W)
        return [
            remote(
                xin.at[span(part * 256 + core * 128, 128), cols],
                xin.at[span(part * 256 + core * 128, 128), cols],
                p_send, p_recv.at[part, j], partner,
            )
            for part in range(2)
        ]

    def relay(j):
        for arrived, copy in zip(x_copies(j), p_copies(j)):
            arrived.wait_recv()
            copy.start()

    def take(j):
        for copy in p_copies(j):
            copy.wait_recv()
        cols = span(j * W, W)
        hi, lo = split(xin[:, cols])
        xhi[span(other * PART, PART), cols] = hi
        xlo[span(other * PART, PART), cols] = lo

    def prepare(i):
        mask = structure[zl, pr * NR + i].astype(F32)
        for col in range(S // 128):
            v = lst[pl.ds(i * rows + col * NSUP + zl, BLK, stride=S * NSUP // 128), :] * mask
            hi, lo = split(v)
            block = span(zl * PART + i * BLK, BLK)
            xhi[block, pl.ds(col * 128, 128)] = hi
            xlo[block, pl.ds(col * 128, 128)] = lo

    def forward(j):
        xx = rem(x + j, NX)
        cols = span(xx * DEPTH, DEPTH)
        await_bytes(mid.at[:, cols], m_recv.at[xx])
        dst = abuf.at[0, span(x * 32, 32)]
        if j:
            remote(mid.at[:, cols], dst, a_send, a_recv.at[x], at_xz(xx, z)).start()
        else:
            pltpu.make_async_copy(mid.at[:, cols], dst, a_recv.at[x]).start()

    def share(xx):
        await_bytes(abuf.at[0, span(xx * 32, 32)], a_recv.at[xx])
        for h, device in enumerate((z_up, z_down)):
            block = span(xx * 32 + h * 16, 16)
            remote(abuf.at[0, block], abuf.at[1, block], n_send, n_recv, device).start()

    def split_rows(g):
        hi, lo = split(abuf[g])
        ahi[g] = hi
        alo[g] = lo

    pack(0)
    send_x(0)

    @pl.loop(1, NCH)
    def _(j):
        pack(j)

    @pl.loop(0, EARLY)
    def _(i):
        prepare(i)

    for j in (1, 2, 3, 0):
        forward(j)
    send_x(1)

    @pl.loop(EARLY, NR)
    def _(i):
        prepare(i)

    relay(0)
    for j in (0, 1, 3, 2):
        share(rem(x + j, NX))
    send_x(2)
    send_x(3)
    relay(1)
    split_rows(0)

    def x_stage(buf, far, final, far_send, far_recv, final_send, final_recv):
        def first(j):
            cols = span(j * W, W)
            return [
                remote(
                    buf.at[span(x_far * 32 + h * 16, 16), cols],
                    far.at[h, :, cols], far_send, far_recv.at[h, j], device,
                )
                for h, device in enumerate((right, left))
            ]

        def second(j):
            cols = span(j * W, W)
            return [
                remote(
                    buf.at[span(target * 32, 32), cols],
                    final.at[h, :, cols], final_send, final_recv.at[h, j], device,
                )
                for h, (device, target) in enumerate(((right, x_next), (left, x_prev)))
            ]

        def send_first(j):
            for copy in first(j):
                copy.start()

        def send_second(j):
            cols = span(j * W, W)
            for h, (copy, target) in enumerate(zip(first(j), (x_next, x_prev))):
                copy.wait_recv()
                buf[span(target * 32 + h * 16, 16), cols] += far[h, :, cols]
            for copy in second(j):
                copy.start()

        def total(j):
            cols = span(j * W, W)
            for copy in second(j):
                copy.wait_recv()
            return buf[span(x * 32, 32), cols] + (final[0, :, cols] + final[1, :, cols])

        return send_first, send_second, total

    y_first, y_second, y_total = x_stage(ybuf, xo, xf, xo_send, xo_recv, xf_send, xf_recv)
    d_first, d_second, d_total = x_stage(dbuf, dxo, dxf, dxo_send, dxo_recv, dxf_send, dxf_recv)

    def item(i):
        g = jnp.where(i < 4, div(i, 2), rem(i, 2))
        c = jnp.where(i < 4, rem(i, 2), div(i, 2))
        return g, c, g * NCH + c

    def first_product(i):
        g, c, j = item(i)
        cols = span(c * W, W)
        ybuf[:, span(j * W, W)] = dot3(ahi[g], alo[g], xhi[:, cols], xlo[:, cols])
        y_first(j)

    def finish_c(i):
        g, c, j = item(i)
        cols = span(j * W, W)
        value = y_total(j)
        for h, neighbour in enumerate((z_down, z_up)):
            owner_row = jnp.where(g == 0, pr, neighbour[0])
            owner_col = jnp.where(g == 0, pc, neighbour[1])
            mask = structure[zl, owner_row * NR + div(owner_col, 2)].astype(F32)
            part = pl.ds(h * 16, 16)
            crow[part, cols] = -mask * value[h * 16 : h * 16 + 16]
            home = span(rem(owner_row, 2) * PART + owner_col * 32 + h * 16, 16)
            for n in range(W // T):
                q = (n // 2) * 8 + ((n % 2) * 2 + rem(c + n // 2, 2)) * 2 + div(c, 2)
                src = crow.at[part, span(j * W + n * T, T)]

                @pl.when(q == pc)
                def _():
                    pltpu.make_async_copy(src, cbuf.at[home], c_recv).start()

                @pl.when(q != pc)
                def _():
                    remote(src, cbuf.at[home], c_send, c_recv, (pr, q)).start()

            @pl.when(g == 1)
            def _():
                remote(crow.at[part, cols], cout.at[part, span(c * W, W)], o_send, o_recv, neighbour).start()

        @pl.when(g == 0)
        def _():
            out_c[:, span(zl * S + c * W, W)] = crow[:, cols]

    @pl.loop(0, ITEMS + LAG2)
    def _(i):
        @pl.when(jnp.logical_or(i < 2, jnp.logical_or(i == 4, i == 6)))
        def _():
            take(jnp.where(i < 2, i, div(i, 2)))

        @pl.when(i == 2)
        def _():
            await_bytes(abuf.at[1], n_recv)
            split_rows(1)

        @pl.when(i < ITEMS)
        def _():
            first_product(i)

        @pl.when(jnp.logical_or(i == 3, i == 5))
        def _():
            relay(div(i, 2) + 1)

        @pl.when(jnp.logical_and(i >= LAG1, i < ITEMS + LAG1))
        def _():
            y_second(item(i - LAG1)[2])

        @pl.when(i >= LAG2)
        def _():
            finish_c(i - LAG2)

    await_bytes(cbuf, c_recv)
    chi, clo = split(cbuf[...].T)

    @pl.loop(0, NCH)
    def _(n):
        cols = span(n * W, W)
        dbuf[:, cols] = dot3(chi, clo, xhi[:, cols], xlo[:, cols])
        d_first(n)

    @pl.loop(0, NCH)
    def _(n):
        d_second(n)

    owner = (2 * core + rem(y + zh, 2)) * 2 + zh

    @pl.loop(0, NCH)
    def _(n):
        dsum[:, span(n * W, W)] = d_total(n)
        for i in range(W // T):
            q = n * (W // T) + i
            src = dsum.at[:, span(q * T, T)]
            dst = dfin.at[zl, span(div(y, 2) * 128 + x * 32, 32)]
            own = jnp.logical_and(owner == pr, q == pc)

            @pl.when(own)
            def _():
                pltpu.make_async_copy(src, dst, d_recv).start()

            @pl.when(jnp.logical_not(own))
            def _():
                remote(src, dst, d_send, d_recv, (owner, q)).start()

    await_bytes(cout, o_recv)
    out_c[:, span(other * S, S)] = cout[...]
    piv_copy.wait()
    await_bytes(dfin, d_recv)
    for k in range(NSUP):
        out_d[k] = piv[k] - dfin[k].T

    await_bytes(abuf.at[0, pl.ds(0, 120)], m_send)
    await_bytes(abuf.at[0, pl.ds(0, 96)], a_send)
    await_bytes(abuf.at[0], n_send)
    await_bytes(xs, x_send)
    await_bytes(xs, p_send)
    await_bytes(xo, xo_send)
    await_bytes(xf, xf_send)
    await_bytes(cbuf.at[pl.ds(0, 960)], c_send)
    await_bytes(cout, o_send)
    await_bytes(dxo, dxo_send)
    await_bytes(dxf, dxf_send)
    await_bytes(cbuf.at[pl.ds(0, 480)], d_send)

    @pl.when(owner != pr)
    def _():
        await_bytes(cbuf.at[pl.ds(0, 32)], d_send)


def body(ancestor_inverse, lower_panel, pivot_inverse, structure):
    panel = lower_panel.reshape(PART, NSUP, S // 128, 128).transpose(0, 2, 1, 3)
    panel = panel.reshape(PART * NSUP * S // 128, 128)
    width = NSUP * S
    vmem = pl.BlockSpec(memory_space=pltpu.VMEM)
    hbm = pl.BlockSpec(memory_space=pltpu.HBM)
    dma = pltpu.SemaphoreType.DMA
    columns, diagonal = pl.pallas_call(
        kernel,
        name="selinv",
        out_shape=(
            jax.ShapeDtypeStruct((32, width), F32),
            jax.ShapeDtypeStruct(pivot_inverse.shape, F32),
        ),
        in_specs=[hbm, hbm, hbm, hbm],
        out_specs=(vmem, vmem),
        scratch_shapes=[
            pltpu.VMEM(pivot_inverse.shape, F32),
            pltpu.SMEM(structure.shape, structure.dtype),
            pltpu.VMEM(panel.shape, F32),
            pltpu.VMEM((256, S), F32),
            pltpu.VMEM((PART, S), F32),
            pltpu.VMEM((DEPTH, S), BF16),
            pltpu.VMEM((DEPTH, S), BF16),
            pltpu.VMEM((32, NX * DEPTH), F32),
            pltpu.VMEM((2, 128, DEPTH), F32),
            pltpu.VMEM((2, 128, DEPTH), BF16),
            pltpu.VMEM((2, 128, DEPTH), BF16),
            pltpu.VMEM((128, width), F32),
            pltpu.VMEM((2, 16, width), F32),
            pltpu.VMEM((2, 32, width), F32),
            pltpu.VMEM((32, width), F32),
            pltpu.VMEM((32, S), F32),
            pltpu.VMEM((DEPTH, T), F32),
            pltpu.VMEM((128, S), F32),
            pltpu.VMEM((2, 16, S), F32),
            pltpu.VMEM((2, 32, S), F32),
            pltpu.VMEM((32, S), F32),
            pltpu.VMEM((NSUP, 256, 128), F32),
            dma(()),
            dma(()),
            dma((NR,)),
            dma(()),
            dma((NX,)),
            dma(()),
            dma((NX,)),
            dma(()),
            dma(()),
            dma(()),
            dma((2, NCH)),
            dma(()),
            dma((2, NCH)),
            dma(()),
            dma((2, ITEMS)),
            dma(()),
            dma((2, ITEMS)),
            dma(()),
            dma(()),
            dma(()),
            dma(()),
            dma(()),
            dma((2, NCH)),
            dma(()),
            dma((2, NCH)),
            dma(()),
            dma(()),
        ],
        compiler_params=pltpu.CompilerParams(
            collective_id=0, has_side_effects=True, vmem_limit_bytes=40 * 2**20
        ),
    )(
        *(
            pltpu.with_memory_space_constraint(v, pltpu.HBM)
            for v in (ancestor_inverse, panel, pivot_inverse, structure)
        )
    )
    return columns.reshape(32, NSUP, S), diagonal


def solution(mesh):
    return jax.shard_map(
        body,
        mesh=mesh,
        in_specs=(P("prow", "pcol"), P("prow", None, None), P(None, "pcol", "prow"), P()),
        out_specs=(P(("prow", "pcol"), None, None), P(None, "pcol", "prow")),
        check_vma=False,
    )
```

```python
import functools

import jax
import jax.numpy as jnp
from jax import lax
from jax.experimental import pallas as pl
from jax.experimental.pallas import tpu as pltpu
from jax.sharding import PartitionSpec as P

MESH = pl.DeviceIdType.MESH
F32 = jnp.float32
BF16 = jnp.bfloat16
S = 2048
NSUP = 2
BLK = 64
NX, NZ = 4, 4
NR, NC = 8, 16
PART = 512
DEPTH = 2 * PART
W = 512
NCH = S // W
ITEMS = 2 * NCH
EARLY = 4
LAG1, LAG2 = 2, 4
DIAG = 12
T = S // NC


def split(v):
    hi = v.astype(BF16)
    return hi, (v - hi.astype(F32)).astype(BF16)


def dot3(ahi, alo, bhi, blo):
    dot = functools.partial(jnp.dot, preferred_element_type=F32)
    return dot(ahi, bhi) + (dot(ahi, blo) + dot(alo, bhi))


def kernel(
    a_hbm, l_hbm, piv_hbm, structure_hbm, out_c, out_d,
    piv, structure, lst, xs, xin, xhi, xlo, mid, abuf, ahi, alo, ybuf, xo, xf,
    crow, cout, cbuf, dbuf, dxo, dxf, dsum, dfin,
    piv_sem, structure_sem, l_sem, m_send, m_recv, a_send, a_recv, n_send, n_recv,
    x_send, x_recv, w_send, p_send, p_recv, xo_send, xo_recv, xf_send, xf_recv,
    c_send, c_recv, o_send, o_recv, dxo_send, dxo_recv, dxf_send, dxf_recv, d_send, d_recv,
):
    rem, div = lax.rem, lax.div
    pr, pc = lax.axis_index("prow"), lax.axis_index("pcol")
    x, zl = div(pr, 2), rem(pr, 2)
    zh, rest = div(pc, 8), rem(pc, 8)
    y, core = div(rest, 2), rem(pc, 2)
    z = 2 * zh + zl
    other = 1 - zl

    def at_xz(xx, zz):
        return (xx * 2 + rem(zz, 2), div(zz, 2) * 8 + rest)

    z_down, z_up = at_xz(x, rem(z + 3, 4)), at_xz(x, rem(z + 1, 4))
    x_next, x_prev, x_far = rem(x + 1, 4), rem(x + 3, 4), rem(x + 2, 4)
    right, left = at_xz(x_next, z), at_xz(x_prev, z)
    partner = (pr, pc + 1 - 2 * core)
    y_up, y_down = ((pr, zh * 8 + rem(y + d, 4) * 2 + core) for d in (1, 3))
    parity = rem(y, 2)

    def chunk(n):
        return n + parity * (1 - 2 * rem(n, 2))

    def remote(src, dst, send, recv, device):
        return pltpu.make_async_remote_copy(
            src_ref=src, dst_ref=dst, send_sem=send, recv_sem=recv,
            device_id=device, device_id_type=MESH,
        )

    def await_bytes(ref, sem):
        pltpu.make_async_copy(ref, ref, sem).wait()

    def span(start, size):
        return pl.ds(pl.multiple_of(start, size), size)

    rows = BLK * NSUP * S // 128
    structure_copy = pltpu.make_async_copy(structure_hbm, structure, structure_sem)
    structure_copy.start()
    for i in range(NR):
        block = pl.ds(i * rows, rows)
        pltpu.make_async_copy(l_hbm.at[block], lst.at[block], l_sem.at[i]).start()
    piv_copy = pltpu.make_async_copy(piv_hbm, piv, piv_sem)
    piv_copy.start()

    barrier = pltpu.get_barrier_semaphore()

    def greet(device):
        pl.semaphore_signal(barrier, inc=1, device_id=device, device_id_type=MESH)

    for j in range(1, NC):
        greet((pr, rem(pc + j, NC)))
    for j in range(1, NX):
        greet(at_xz(rem(x + j, NX), z))
    greet(z_down)
    greet(z_up)
    pl.semaphore_wait(barrier, NC - 1 + NX - 1 + 2)

    def a_piece(q):
        src = a_hbm.at[span(q * 32, 32)]
        return src, mid.at[:, span(pc * 256, 256)], m_recv.at[div(pc, 4)]

    pltpu.make_async_copy(*a_piece(pc)).start()

    @pl.loop(1, NC)
    def _(j):
        q = rem(pc + j, NC)
        src, dst, recv = a_piece(q)
        remote(src, dst, m_send, recv, (pr, q)).start()

    structure_copy.wait()
    for i in range(NR):
        block = pl.ds(i * rows, rows)
        pltpu.make_async_copy(l_hbm.at[block], lst.at[block], l_sem.at[i]).wait()

    def pack(j):
        for part in range(2):
            for b in range(2):
                i = part * 4 + 2 * core + b
                mask = structure[other, pr * NR + i].astype(F32)
                for col in range(W // 128):
                    first = i * rows + (j * (W // 128) + col) * NSUP + other
                    v = lst[pl.ds(first, BLK, stride=S * NSUP // 128), :]
                    xs[pl.ds(part * 128 + b * BLK, BLK), span((j * (W // 128) + col) * 128, 128)] = v * mask

    def x_copies(j):
        cols = span(j * W, W)
        return [
            remote(
                xs.at[pl.ds(part * 128, 128), cols],
                xin.at[span(part * 256 + core * 128, 128), cols],
                x_send, x_recv.at[part, j], device,
            )
            for part, device in enumerate((z_up, z_down))
        ]

    def send_x(j):
        for copy in x_copies(j):
            copy.start()

    def p_copies(j):
        cols = span(j * W, W)
        return [
            remote(
                xin.at[span(part * 256 + core * 128, 128), cols],
                xin.at[span(part * 256 + core * 128, 128), cols],
                p_send, p_recv.at[part, j], partner,
            )
            for part in range(2)
        ]

    def relay(j, pass_on):
        cols = span(j * W, W)
        for part, (arrived, copy) in enumerate(zip(x_copies(j), p_copies(j))):
            arrived.wait_recv()
            if pass_on:
                block = xin.at[span(part * 256 + core * 128, 128), cols]
                remote(block, block, w_send, x_recv.at[part, j], (y_up, y_down)[part]).start()
            copy.start()

    def take(j):
        for copy in p_copies(j):
            copy.wait_recv()
        cols = span(j * W, W)
        hi, lo = split(xin[:, cols])
        xhi[span(other * PART, PART), cols] = hi
        xlo[span(other * PART, PART), cols] = lo

    def prepare(i):
        mask = structure[zl, pr * NR + i].astype(F32)
        for col in range(S // 128):
            v = lst[pl.ds(i * rows + col * NSUP + zl, BLK, stride=S * NSUP // 128), :] * mask
            hi, lo = split(v)
            block = span(zl * PART + i * BLK, BLK)
            xhi[block, pl.ds(col * 128, 128)] = hi
            xlo[block, pl.ds(col * 128, 128)] = lo

    def forward(j):
        xx = rem(x + j, NX)
        cols = span(xx * DEPTH, DEPTH)
        await_bytes(mid.at[:, cols], m_recv.at[xx])
        dst = abuf.at[0, span(x * 32, 32)]
        if j:
            remote(mid.at[:, cols], dst, a_send, a_recv.at[x], at_xz(xx, z)).start()
        else:
            pltpu.make_async_copy(mid.at[:, cols], dst, a_recv.at[x]).start()

    def share(xx):
        await_bytes(abuf.at[0, span(xx * 32, 32)], a_recv.at[xx])
        for h, device in enumerate((z_up, z_down)):
            block = span(xx * 32 + h * 16, 16)
            remote(abuf.at[0, block], abuf.at[1, block], n_send, n_recv, device).start()

    def split_rows(g):
        hi, lo = split(abuf[g])
        ahi[g] = hi
        alo[g] = lo

    for n in (0, 2):
        pack(chunk(n))
        send_x(chunk(n))

    @pl.loop(0, EARLY)
    def _(i):
        prepare(i)

    for j in (1, 2, 3, 0):
        forward(j)

    @pl.loop(EARLY, NR)
    def _(i):
        prepare(i)

    relay(chunk(0), True)
    for j in (0, 1, 3, 2):
        share(rem(x + j, NX))
    split_rows(0)

    def x_stage(buf, far, final, far_send, far_recv, final_send, final_recv):
        def first(j):
            cols = span(j * W, W)
            return [
                remote(
                    buf.at[span(x_far * 32 + h * 16, 16), cols],
                    far.at[h, :, cols], far_send, far_recv.at[h, j], device,
                )
                for h, device in enumerate((right, left))
            ]

        def second(j):
            cols = span(j * W, W)
            return [
                remote(
                    buf.at[span(target * 32, 32), cols],
                    final.at[h, :, cols], final_send, final_recv.at[h, j], device,
                )
                for h, (device, target) in enumerate(((right, x_next), (left, x_prev)))
            ]

        def send_first(j):
            for copy in first(j):
                copy.start()

        def send_second(j):
            cols = span(j * W, W)
            for h, (copy, target) in enumerate(zip(first(j), (x_next, x_prev))):
                copy.wait_recv()
                buf[span(target * 32 + h * 16, 16), cols] += far[h, :, cols]
            for copy in second(j):
                copy.start()

        def total(j):
            cols = span(j * W, W)
            for copy in second(j):
                copy.wait_recv()
            return buf[span(x * 32, 32), cols] + (final[0, :, cols] + final[1, :, cols])

        return send_first, send_second, total

    y_first, y_second, y_total = x_stage(ybuf, xo, xf, xo_send, xo_recv, xf_send, xf_recv)
    d_first, d_second, d_total = x_stage(dbuf, dxo, dxf, dxo_send, dxo_recv, dxf_send, dxf_recv)

    def item(i):
        own = jnp.logical_or(i < 3, i == 5)
        g = jnp.where(own, 0, 1)
        n = jnp.where(i < 3, rem(2 * i, 3), jnp.where(i < 5, i - 3, jnp.where(i == 5, 3, i - 4)))
        c = chunk(n)
        return g, c, g * NCH + c

    def first_product(i):
        g, c, j = item(i)
        cols = span(c * W, W)
        ybuf[:, span(j * W, W)] = dot3(ahi[g], alo[g], xhi[:, cols], xlo[:, cols])
        y_first(j)

    def finish_c(i):
        g, c, j = item(i)
        cols = span(j * W, W)
        value = y_total(j)
        for h, neighbour in enumerate((z_down, z_up)):
            owner_row = jnp.where(g == 0, pr, neighbour[0])
            owner_col = jnp.where(g == 0, pc, neighbour[1])
            mask = structure[zl, owner_row * NR + div(owner_col, 2)].astype(F32)
            part = pl.ds(h * 16, 16)
            crow[part, cols] = -mask * value[h * 16 : h * 16 + 16]
            home = span(rem(owner_row, 2) * PART + owner_col * 32 + h * 16, 16)
            for n in range(W // T):
                q = (n // 2) * 8 + ((n % 2) * 2 + rem(c + n // 2, 2)) * 2 + div(c, 2)
                src = crow.at[part, span(j * W + n * T, T)]

                @pl.when(q == pc)
                def _():
                    pltpu.make_async_copy(src, cbuf.at[home], c_recv).start()

                @pl.when(q != pc)
                def _():
                    remote(src, cbuf.at[home], c_send, c_recv, (pr, q)).start()

            @pl.when(g == 1)
            def _():
                remote(crow.at[part, cols], cout.at[part, span(c * W, W)], o_send, o_recv, neighbour).start()

        @pl.when(g == 0)
        def _():
            out_c[:, span(zl * S + c * W, W)] = crow[:, cols]

    def turned(n):
        return rem(n + y, NCH)

    def second_product():
        await_bytes(cbuf, c_recv)
        chi, clo = split(cbuf[...].T)

        @pl.loop(0, NCH)
        def _(i):
            n = turned(i)
            cols = span(n * W, W)
            dbuf[:, cols] = dot3(chi, clo, xhi[:, cols], xlo[:, cols])
            d_first(n)

    def second_ring():
        @pl.loop(0, NCH)
        def _(n):
            d_second(turned(n))

    @pl.loop(0, 14)
    def _(i):
        @pl.when(jnp.logical_or(i < 3, i == 5))
        def _():
            take(item(i)[1])

        @pl.when(i == 3)
        def _():
            await_bytes(abuf.at[1], n_recv)
            split_rows(1)

        @pl.when(i < ITEMS)
        def _():
            first_product(i)

        @pl.when(i == 0)
        def _():
            relay(chunk(2), True)

        @pl.when(jnp.logical_or(i == 1, i == 3))
        def _():
            relay(chunk(i), False)

        @pl.when(jnp.logical_and(i >= LAG1, i < ITEMS + LAG1))
        def _():
            y_second(item(i - LAG1)[2])

        @pl.when(jnp.logical_and(i >= LAG2, i < ITEMS + LAG2))
        def _():
            finish_c(i - LAG2)

        @pl.when(jnp.logical_and(i == DIAG, core == 0))
        def _():
            second_product()

        @pl.when(jnp.logical_and(i == DIAG + 1, core == 0))
        def _():
            second_ring()

    @pl.when(core == 1)
    def _():
        second_product()
        second_ring()

    owner = (2 * core + rem(y + zh, 2)) * 2 + zh

    @pl.loop(0, NCH)
    def _(j):
        n = turned(j)
        dsum[:, span(n * W, W)] = d_total(n)
        for i in range(W // T):
            q = n * (W // T) + i
            src = dsum.at[:, span(q * T, T)]
            dst = dfin.at[zl, span(div(y, 2) * 128 + x * 32, 32)]
            own = jnp.logical_and(owner == pr, q == pc)

            @pl.when(own)
            def _():
                pltpu.make_async_copy(src, dst, d_recv).start()

            @pl.when(jnp.logical_not(own))
            def _():
                remote(src, dst, d_send, d_recv, (owner, q)).start()

    await_bytes(cout, o_recv)
    out_c[:, span(other * S, S)] = cout[...]
    piv_copy.wait()
    await_bytes(dfin, d_recv)
    for k in range(NSUP):
        out_d[k] = piv[k] - dfin[k].T

    await_bytes(abuf.at[0, pl.ds(0, 120)], m_send)
    await_bytes(abuf.at[0, pl.ds(0, 96)], a_send)
    await_bytes(abuf.at[0], n_send)
    await_bytes(xs.at[pl.ds(0, 128)], x_send)
    await_bytes(xs.at[pl.ds(0, 128)], w_send)
    await_bytes(xs, p_send)
    await_bytes(xo, xo_send)
    await_bytes(xf, xf_send)
    await_bytes(cbuf.at[pl.ds(0, 960)], c_send)
    await_bytes(cout, o_send)
    await_bytes(dxo, dxo_send)
    await_bytes(dxf, dxf_send)
    await_bytes(cbuf.at[pl.ds(0, 480)], d_send)

    @pl.when(owner != pr)
    def _():
        await_bytes(cbuf.at[pl.ds(0, 32)], d_send)


def body(ancestor_inverse, lower_panel, pivot_inverse, structure):
    panel = lower_panel.reshape(PART, NSUP, S // 128, 128).transpose(0, 2, 1, 3)
    panel = panel.reshape(PART * NSUP * S // 128, 128)
    width = NSUP * S
    vmem = pl.BlockSpec(memory_space=pltpu.VMEM)
    hbm = pl.BlockSpec(memory_space=pltpu.HBM)
    dma = pltpu.SemaphoreType.DMA
    columns, diagonal = pl.pallas_call(
        kernel,
        name="selinv",
        out_shape=(
            jax.ShapeDtypeStruct((32, width), F32),
            jax.ShapeDtypeStruct(pivot_inverse.shape, F32),
        ),
        in_specs=[hbm, hbm, hbm, hbm],
        out_specs=(vmem, vmem),
        scratch_shapes=[
            pltpu.VMEM(pivot_inverse.shape, F32),
            pltpu.SMEM(structure.shape, structure.dtype),
            pltpu.VMEM(panel.shape, F32),
            pltpu.VMEM((256, S), F32),
            pltpu.VMEM((PART, S), F32),
            pltpu.VMEM((DEPTH, S), BF16),
            pltpu.VMEM((DEPTH, S), BF16),
            pltpu.VMEM((32, NX * DEPTH), F32),
            pltpu.VMEM((2, 128, DEPTH), F32),
            pltpu.VMEM((2, 128, DEPTH), BF16),
            pltpu.VMEM((2, 128, DEPTH), BF16),
            pltpu.VMEM((128, width), F32),
            pltpu.VMEM((2, 16, width), F32),
            pltpu.VMEM((2, 32, width), F32),
            pltpu.VMEM((32, width), F32),
            pltpu.VMEM((32, S), F32),
            pltpu.VMEM((DEPTH, T), F32),
            pltpu.VMEM((128, S), F32),
            pltpu.VMEM((2, 16, S), F32),
            pltpu.VMEM((2, 32, S), F32),
            pltpu.VMEM((32, S), F32),
            pltpu.VMEM((NSUP, 256, 128), F32),
            dma(()),
            dma(()),
            dma((NR,)),
            dma(()),
            dma((NX,)),
            dma(()),
            dma((NX,)),
            dma(()),
            dma(()),
            dma(()),
            dma((2, NCH)),
            dma(()),
            dma(()),
            dma((2, NCH)),
            dma(()),
            dma((2, ITEMS)),
            dma(()),
            dma((2, ITEMS)),
            dma(()),
            dma(()),
            dma(()),
            dma(()),
            dma(()),
            dma((2, NCH)),
            dma(()),
            dma((2, NCH)),
            dma(()),
            dma(()),
        ],
        compiler_params=pltpu.CompilerParams(
            collective_id=0, has_side_effects=True, vmem_limit_bytes=40 * 2**20
        ),
    )(
        *(
            pltpu.with_memory_space_constraint(v, pltpu.HBM)
            for v in (ancestor_inverse, panel, pivot_inverse, structure)
        )
    )
    return columns.reshape(32, NSUP, S), diagonal


def solution(mesh):
    return jax.shard_map(
        body,
        mesh=mesh,
        in_specs=(P("prow", "pcol"), P("prow", None, None), P(None, "pcol", "prow"), P()),
        out_specs=(P(("prow", "pcol"), None, None), P(None, "pcol", "prow")),
        check_vma=False,
    )
```

```python
import functools

import jax
import jax.numpy as jnp
from jax import lax
from jax.experimental import pallas as pl
from jax.experimental.pallas import tpu as pltpu
from jax.sharding import PartitionSpec as P

MESH = pl.DeviceIdType.MESH
F32 = jnp.float32
BF16 = jnp.bfloat16
S = 2048
NSUP = 2
BLK = 64
NX, NZ = 4, 4
NR, NC = 8, 16
PART = 512
DEPTH = 2 * PART
W = 512
NCH = S // W
ITEMS = 2 * NCH
EARLY = 5
LAG1, LAG2 = 2, 4
H = W // 2
T = S // NC


def split(v):
    hi = v.astype(BF16)
    return hi, (v - hi.astype(F32)).astype(BF16)


def dot3(ahi, alo, bhi, blo):
    dot = functools.partial(jnp.dot, preferred_element_type=F32)
    return dot(ahi, bhi) + (dot(ahi, blo) + dot(alo, bhi))


def kernel(
    a_hbm, l_hbm, piv_hbm, structure_hbm, out_c, out_d,
    piv, structure, lst, xs, xin, xhi, xlo, mid, abuf, ahi, alo, ybuf, xo, xf,
    crow, cout, cbuf, dbuf, dxo, dxf, dsum, dfin,
    piv_sem, structure_sem, l_sem, m_send, m_recv, a_send, a_recv, n_send, n_recv,
    x_send, x_recv, w_send, p_send, p_recv, xo_send, xo_recv, xf_send, xf_recv,
    c_send, c_recv, o_send, o_recv, dxo_send, dxo_recv, dxf_send, dxf_recv, d_send, d_recv,
):
    rem, div = lax.rem, lax.div
    pr, pc = lax.axis_index("prow"), lax.axis_index("pcol")
    x, zl = div(pr, 2), rem(pr, 2)
    zh, rest = div(pc, 8), rem(pc, 8)
    y, core = div(rest, 2), rem(pc, 2)
    z = 2 * zh + zl
    other = 1 - zl

    def at_xz(xx, zz):
        return (xx * 2 + rem(zz, 2), div(zz, 2) * 8 + rest)

    z_down, z_up = at_xz(x, rem(z + 3, 4)), at_xz(x, rem(z + 1, 4))
    x_next, x_prev, x_far = rem(x + 1, 4), rem(x + 3, 4), rem(x + 2, 4)
    right, left = at_xz(x_next, z), at_xz(x_prev, z)
    partner = (pr, pc + 1 - 2 * core)
    y_up, y_down = ((pr, zh * 8 + rem(y + d, 4) * 2 + core) for d in (1, 3))
    parity = rem(y, 2)

    def chunk(n):
        return n + parity * (1 - 2 * rem(n, 2))

    def remote(src, dst, send, recv, device):
        return pltpu.make_async_remote_copy(
            src_ref=src, dst_ref=dst, send_sem=send, recv_sem=recv,
            device_id=device, device_id_type=MESH,
        )

    def await_bytes(ref, sem):
        pltpu.make_async_copy(ref, ref, sem).wait()

    def span(start, size):
        return pl.ds(pl.multiple_of(start, size), size)

    rows = BLK * NSUP * S // 128
    structure_copy = pltpu.make_async_copy(structure_hbm, structure, structure_sem)
    structure_copy.start()
    for i in range(NR):
        block = pl.ds(i * rows, rows)
        pltpu.make_async_copy(l_hbm.at[block], lst.at[block], l_sem.at[i]).start()
    piv_copy = pltpu.make_async_copy(piv_hbm, piv, piv_sem)
    piv_copy.start()

    barrier = pltpu.get_barrier_semaphore()

    def greet(device):
        pl.semaphore_signal(barrier, inc=1, device_id=device, device_id_type=MESH)

    for j in range(1, NC):
        greet((pr, rem(pc + j, NC)))
    for j in range(1, NX):
        greet(at_xz(rem(x + j, NX), z))
    greet(z_down)
    greet(z_up)
    pl.semaphore_wait(barrier, NC - 1 + NX - 1 + 2)

    def a_piece(q, h):
        src = a_hbm.at[span(q * 32 + h * 16, 16)]
        return src, mid.at[pl.ds(h * 16, 16), span(pc * 256, 256)], m_recv.at[h, div(pc, 4)]

    for h in range(2):
        pltpu.make_async_copy(*a_piece(pc, h)).start()

        @pl.loop(1, NC)
        def _(j):
            q = rem(pc + j, NC)
            src, dst, recv = a_piece(q, h)
            remote(src, dst, m_send, recv, (pr, q)).start()

    structure_copy.wait()
    for i in range(NR):
        block = pl.ds(i * rows, rows)
        pltpu.make_async_copy(l_hbm.at[block], lst.at[block], l_sem.at[i]).wait()

    def pack(j):
        for part in range(2):
            for b in range(2):
                i = part * 4 + 2 * core + b
                mask = structure[other, pr * NR + i].astype(F32)
                for col in range(W // 128):
                    first = i * rows + (j * (W // 128) + col) * NSUP + other
                    v = lst[pl.ds(first, BLK, stride=S * NSUP // 128), :]
                    xs[pl.ds(part * 128 + b * BLK, BLK), span((j * (W // 128) + col) * 128, 128)] = v * mask

    def x_copies(j, half):
        cols = span(j * W + half * H, H)
        return [
            remote(
                xs.at[pl.ds(part * 128, 128), cols],
                xin.at[span(part * 256 + core * 128, 128), cols],
                x_send, x_recv.at[part, 2 * j + half], device,
            )
            for part, device in enumerate((z_up, z_down))
        ]

    def send_x(j):
        for half in range(2):
            for copy in x_copies(j, half):
                copy.start()

    def p_copies(j, half):
        cols = span(j * W + half * H, H)
        return [
            remote(
                xin.at[span(part * 256 + core * 128, 128), cols],
                xin.at[span(part * 256 + core * 128, 128), cols],
                p_send, p_recv.at[part, 2 * j + half], partner,
            )
            for part in range(2)
        ]

    def relay(j, half, pass_on):
        cols = span(j * W + half * H, H)
        for part, (arrived, copy) in enumerate(zip(x_copies(j, half), p_copies(j, half))):
            arrived.wait_recv()
            if pass_on:
                block = xin.at[span(part * 256 + core * 128, 128), cols]
                remote(block, block, w_send, x_recv.at[part, 2 * j + half], (y_up, y_down)[part]).start()
            copy.start()

    def take(j):
        for half in range(2):
            for copy in p_copies(j, half):
                copy.wait_recv()
        cols = span(j * W, W)
        hi, lo = split(xin[:, cols])
        xhi[span(other * PART, PART), cols] = hi
        xlo[span(other * PART, PART), cols] = lo

    def prepare(i):
        mask = structure[zl, pr * NR + i].astype(F32)
        for col in range(S // 128):
            v = lst[pl.ds(i * rows + col * NSUP + zl, BLK, stride=S * NSUP // 128), :] * mask
            hi, lo = split(v)
            block = span(zl * PART + i * BLK, BLK)
            xhi[block, pl.ds(col * 128, 128)] = hi
            xlo[block, pl.ds(col * 128, 128)] = lo

    def forward(h):
        for j in (1, 2, 3, 0):
            xx = rem(x + j, NX)
            src = mid.at[pl.ds(h * 16, 16), span(xx * DEPTH, DEPTH)]
            await_bytes(src, m_recv.at[h, xx])
            dst, recv = abuf.at[0, span(x * 32 + h * 16, 16)], a_recv.at[h, x]
            if j:
                remote(src, dst, a_send, recv, at_xz(xx, z)).start()
            else:
                pltpu.make_async_copy(src, dst, recv).start()

    def share(h):
        for j in (0, 1, 3, 2):
            xx = rem(x + j, NX)
            block = span(xx * 32 + h * 16, 16)
            await_bytes(abuf.at[0, block], a_recv.at[h, xx])
            remote(abuf.at[0, block], abuf.at[1, block], n_send, n_recv, (z_up, z_down)[h]).start()

    def split_rows(g):
        hi, lo = split(abuf[g])
        ahi[g] = hi
        alo[g] = lo

    for n in (0, 2):
        pack(chunk(n))
        send_x(chunk(n))

    @pl.loop(0, EARLY)
    def _(i):
        prepare(i)

    forward(0)

    @pl.loop(EARLY, NR)
    def _(i):
        prepare(i)

    forward(1)
    share(0)
    relay(chunk(0), 0, True)
    share(1)
    relay(chunk(0), 1, True)
    split_rows(0)

    def x_stage(buf, far, final, far_send, far_recv, final_send, final_recv):
        def first(j):
            cols = span(j * W, W)
            return [
                remote(
                    buf.at[span(x_far * 32 + h * 16, 16), cols],
                    far.at[h, :, cols], far_send, far_recv.at[h, j], device,
                )
                for h, device in enumerate((right, left))
            ]

        def second(j):
            cols = span(j * W, W)
            return [
                remote(
                    buf.at[span(target * 32, 32), cols],
                    final.at[h, :, cols], final_send, final_recv.at[h, j], device,
                )
                for h, (device, target) in enumerate(((right, x_next), (left, x_prev)))
            ]

        def send_first(j):
            for copy in first(j):
                copy.start()

        def send_second(j):
            cols = span(j * W, W)
            for h, (copy, target) in enumerate(zip(first(j), (x_next, x_prev))):
                copy.wait_recv()
                buf[span(target * 32 + h * 16, 16), cols] += far[h, :, cols]
            for copy in second(j):
                copy.start()

        def total(j):
            cols = span(j * W, W)
            for copy in second(j):
                copy.wait_recv()
            return buf[span(x * 32, 32), cols] + (final[0, :, cols] + final[1, :, cols])

        return send_first, send_second, total

    y_first, y_second, y_total = x_stage(ybuf, xo, xf, xo_send, xo_recv, xf_send, xf_recv)
    d_first, d_second, d_total = x_stage(dbuf, dxo, dxf, dxo_send, dxo_recv, dxf_send, dxf_recv)

    def item(i):
        own = jnp.logical_or(i < 3, i == 5)
        g = jnp.where(own, 0, 1)
        n = jnp.where(i < 3, rem(2 * i, 3), jnp.where(i < 5, i - 3, jnp.where(i == 5, 3, i - 4)))
        c = chunk(n)
        return g, c, g * NCH + c

    def first_product(i):
        g, c, j = item(i)
        cols = span(c * W, W)
        ybuf[:, span(j * W, W)] = dot3(ahi[g], alo[g], xhi[:, cols], xlo[:, cols])
        y_first(j)

    def finish_c(i):
        g, c, j = item(i)
        cols = span(j * W, W)
        value = y_total(j)
        for h, neighbour in enumerate((z_down, z_up)):
            owner_row = jnp.where(g == 0, pr, neighbour[0])
            owner_col = jnp.where(g == 0, pc, neighbour[1])
            mask = structure[zl, owner_row * NR + div(owner_col, 2)].astype(F32)
            part = pl.ds(h * 16, 16)
            crow[part, cols] = -mask * value[h * 16 : h * 16 + 16]
            home = span(rem(owner_row, 2) * PART + owner_col * 32 + h * 16, 16)
            for n in range(W // T):
                q = (n // 2) * 8 + ((n % 2) * 2 + rem(c + n // 2, 2)) * 2 + div(c, 2)
                src = crow.at[part, span(j * W + n * T, T)]

                @pl.when(q == pc)
                def _():
                    pltpu.make_async_copy(src, cbuf.at[home], c_recv.at[g]).start()

                @pl.when(q != pc)
                def _():
                    remote(src, cbuf.at[home], c_send, c_recv.at[g], (pr, q)).start()

            @pl.when(g == 1)
            def _():
                remote(crow.at[part, cols], cout.at[part, span(c * W, W)], o_send, o_recv, neighbour).start()

        @pl.when(g == 0)
        def _():
            for n in range(W // 128):
                place = pl.ds((c * (W // 128) + n) * NSUP + zl, 32, stride=NSUP * S // 128)
                out_c[place, :] = crow[:, span(j * W + n * 128, 128)]

    owner_x = 2 * core + rem(y + zh, 2)
    owner = owner_x * 2 + zh

    def tile_y(target):
        return rem(y + 6 - owner_x + target, 4)

    def second_product(g):
        block = span((zl if g == 0 else other) * PART, PART)
        await_bytes(cbuf.at[block], c_recv.at[g])
        chi, clo = split(cbuf[block, :].T)
        for d in (2, 1, 3, 0):
            target = rem(x + d, NX)
            for b in range(2):
                cols = span(b * (S // 2) + tile_y(target) * 256, 256)
                value = dot3(chi, clo, xhi[block, cols], xlo[block, cols])
                for u in range(NCH):
                    part = span(target * 32, 32), pl.ds(u * W + b * 256, 256)
                    if g == 0:
                        dbuf[part] = value[u * 32 : u * 32 + 32]
                    else:
                        dbuf[part] += value[u * 32 : u * 32 + 32]
            if g == 1 and d == 2:
                for u in range(NCH):
                    d_first(u)

    def second_ring():
        @pl.loop(0, NCH)
        def _(n):
            d_second(n)

    def pass_on(n, onward):
        for half in range(2):
            relay(chunk(n), half, onward)

    take(chunk(0))
    first_product(0)
    pass_on(2, True)
    y_second(item(0)[2])
    pass_on(1, False)
    take(chunk(2))
    first_product(1)
    take(chunk(1))
    first_product(2)
    y_second(item(1)[2])
    finish_c(0)
    await_bytes(abuf.at[1], n_recv)
    split_rows(1)
    first_product(3)
    y_second(item(2)[2])
    pass_on(3, False)

    @pl.loop(4, ITEMS + LAG2)
    def _(i):
        @pl.when(i == 5)
        def _():
            take(chunk(3))

        @pl.when(i < ITEMS)
        def _():
            first_product(i)

        @pl.when(jnp.logical_and(i >= 3 + LAG1, i < ITEMS + LAG1))
        def _():
            y_second(item(i - LAG1)[2])

        @pl.when(i >= 1 + LAG2)
        def _():
            finish_c(i - LAG2)

    second_product(0)
    second_product(1)
    second_ring()

    @pl.loop(0, NCH)
    def _(u):
        dsum[:, span(u * W, W)] = d_total(u)
        for n in range(W // T):
            q = (n // 2) * 8 + tile_y(x) * 2 + n % 2
            src = dsum.at[:, span(u * W + n * T, T)]
            dst = dfin.at[zl, span(div(y, 2) * 128 + u * 32, 32)]
            remote(src, dst, d_send, d_recv, (owner, q)).start()

    await_bytes(cout, o_recv)
    for n in range(S // 128):
        out_c[pl.ds(n * NSUP + other, 32, stride=NSUP * S // 128), :] = cout[:, pl.ds(n * 128, 128)]
    await_bytes(abuf.at[0, pl.ds(0, 120)], m_send)
    await_bytes(abuf.at[0, pl.ds(0, 96)], a_send)
    await_bytes(abuf.at[0], n_send)
    await_bytes(xs.at[pl.ds(0, 128)], x_send)
    await_bytes(xs.at[pl.ds(0, 128)], w_send)
    await_bytes(xs, p_send)
    await_bytes(xo, xo_send)
    await_bytes(xf, xf_send)
    await_bytes(cbuf.at[pl.ds(0, 960)], c_send)
    await_bytes(cout, o_send)
    await_bytes(dxo, dxo_send)
    await_bytes(dxf, dxf_send)
    await_bytes(cbuf.at[pl.ds(0, 512)], d_send)

    piv_copy.wait()
    await_bytes(dfin, d_recv)
    for k in range(NSUP):
        out_d[k] = piv[k] - dfin[k].T


def place(columns, diagonal, out_c, out_d, sem):
    copies = [
        pltpu.make_async_copy(columns, out_c, sem.at[0]),
        pltpu.make_async_copy(diagonal, out_d, sem.at[1]),
    ]
    for copy in copies:
        copy.start()
    for copy in copies:
        copy.wait()


def body(ancestor_inverse, lower_panel, pivot_inverse, structure):
    panel = lower_panel.reshape(PART, NSUP, S // 128, 128).transpose(0, 2, 1, 3)
    panel = panel.reshape(PART * NSUP * S // 128, 128)
    width = NSUP * S
    vmem = pl.BlockSpec(memory_space=pltpu.VMEM)
    hbm = pl.BlockSpec(memory_space=pltpu.HBM)
    dma = pltpu.SemaphoreType.DMA
    columns, diagonal = pl.pallas_call(
        kernel,
        name="selinv",
        out_shape=(
            jax.ShapeDtypeStruct((32 * width // 128, 128), F32),
            jax.ShapeDtypeStruct(pivot_inverse.shape, F32),
        ),
        in_specs=[hbm, hbm, hbm, hbm],
        out_specs=(vmem, vmem),
        scratch_shapes=[
            pltpu.VMEM(pivot_inverse.shape, F32),
            pltpu.SMEM(structure.shape, structure.dtype),
            pltpu.VMEM(panel.shape, F32),
            pltpu.VMEM((256, S), F32),
            pltpu.VMEM((PART, S), F32),
            pltpu.VMEM((DEPTH, S), BF16),
            pltpu.VMEM((DEPTH, S), BF16),
            pltpu.VMEM((32, NX * DEPTH), F32),
            pltpu.VMEM((2, 128, DEPTH), F32),
            pltpu.VMEM((2, 128, DEPTH), BF16),
            pltpu.VMEM((2, 128, DEPTH), BF16),
            pltpu.VMEM((128, width), F32),
            pltpu.VMEM((2, 16, width), F32),
            pltpu.VMEM((2, 32, width), F32),
            pltpu.VMEM((32, width), F32),
            pltpu.VMEM((32, S), F32),
            pltpu.VMEM((DEPTH, T), F32),
            pltpu.VMEM((128, S), F32),
            pltpu.VMEM((2, 16, S), F32),
            pltpu.VMEM((2, 32, S), F32),
            pltpu.VMEM((32, S), F32),
            pltpu.VMEM((NSUP, 256, 128), F32),
            dma(()),
            dma(()),
            dma((NR,)),
            dma(()),
            dma((2, NX)),
            dma(()),
            dma((2, NX)),
            dma(()),
            dma(()),
            dma(()),
            dma((2, 2 * NCH)),
            dma(()),
            dma(()),
            dma((2, 2 * NCH)),
            dma(()),
            dma((2, ITEMS)),
            dma(()),
            dma((2, ITEMS)),
            dma(()),
            dma((2,)),
            dma(()),
            dma(()),
            dma(()),
            dma((2, NCH)),
            dma(()),
            dma((2, NCH)),
            dma(()),
            dma(()),
        ],
        compiler_params=pltpu.CompilerParams(
            collective_id=0, has_side_effects=True, vmem_limit_bytes=40 * 2**20
        ),
    )(
        *(
            pltpu.with_memory_space_constraint(v, pltpu.HBM)
            for v in (ancestor_inverse, panel, pivot_inverse, structure)
        )
    )
    columns, diagonal = pl.pallas_call(
        place,
        name="place",
        out_shape=(
            jax.ShapeDtypeStruct(columns.shape, F32),
            jax.ShapeDtypeStruct(diagonal.shape, F32),
        ),
        in_specs=[vmem, vmem],
        out_specs=(hbm, hbm),
        scratch_shapes=[dma((2,))],
        compiler_params=pltpu.CompilerParams(vmem_limit_bytes=2**20),
    )(columns, diagonal)
    columns = columns.reshape(32, S // 128, NSUP, 128).transpose(0, 2, 1, 3)
    return columns.reshape(32, NSUP, S), diagonal


def solution(mesh):
    return jax.shard_map(
        body,
        mesh=mesh,
        in_specs=(P("prow", "pcol"), P("prow", None, None), P(None, "pcol", "prow"), P()),
        out_specs=(P(("prow", "pcol"), None, None), P(None, "pcol", "prow")),
        check_vma=False,
    )
```

```python
import functools

import jax
import jax.numpy as jnp
from jax import lax
from jax.experimental import pallas as pl
from jax.experimental.pallas import tpu as pltpu
from jax.sharding import PartitionSpec as P

MESH = pl.DeviceIdType.MESH
F32 = jnp.float32
BF16 = jnp.bfloat16
S = 2048
NSUP = 2
BLK = 64
NX, NZ = 4, 4
NR, NC = 8, 16
PART = 512
DEPTH = 2 * PART
W = 512
NCH = S // W
ITEMS = 2 * NCH
EARLY = 5
H = W // 2
T = S // NC


def split(v):
    hi = v.astype(BF16)
    return hi, (v - hi.astype(F32)).astype(BF16)


def dot3(ahi, alo, bhi, blo):
    dot = functools.partial(jnp.dot, preferred_element_type=F32)
    return dot(ahi, bhi) + (dot(ahi, blo) + dot(alo, bhi))


def kernel(
    a_hbm, l_hbm, piv_hbm, structure_hbm, out_c, out_d,
    piv, structure, lst, xs, xin, xhi, xlo, mid, abuf, ahi, alo, ybuf, xo, xf,
    crow, cout, cbuf, dbuf, dxo, dxf, dsum, dfin,
    piv_sem, structure_sem, l_sem, m_send, m_recv, a_send, a_recv, n_send, n_recv,
    x_send, x_recv, w_send, p_send, p_recv, xo_send, xo_recv, xf_send, xf_recv,
    c_send, c_recv, o_send, o_recv, dxo_send, dxo_recv, dxf_send, dxf_recv, d_send, d_recv,
):
    rem, div = lax.rem, lax.div
    pr, pc = lax.axis_index("prow"), lax.axis_index("pcol")
    x, zl = div(pr, 2), rem(pr, 2)
    zh, rest = div(pc, 8), rem(pc, 8)
    y, core = div(rest, 2), rem(pc, 2)
    z = 2 * zh + zl
    other = 1 - zl

    def at_xz(xx, zz):
        return (xx * 2 + rem(zz, 2), div(zz, 2) * 8 + rest)

    z_down, z_up = at_xz(x, rem(z + 3, 4)), at_xz(x, rem(z + 1, 4))
    x_next, x_prev, x_far = rem(x + 1, 4), rem(x + 3, 4), rem(x + 2, 4)
    right, left = at_xz(x_next, z), at_xz(x_prev, z)
    partner = (pr, pc + 1 - 2 * core)
    y_up, y_down = ((pr, zh * 8 + rem(y + d, 4) * 2 + core) for d in (1, 3))
    parity = rem(y, 2)

    def chunk(n):
        return n + parity * (1 - 2 * rem(n, 2))

    def remote(src, dst, send, recv, device):
        return pltpu.make_async_remote_copy(
            src_ref=src, dst_ref=dst, send_sem=send, recv_sem=recv,
            device_id=device, device_id_type=MESH,
        )

    def await_bytes(ref, sem):
        pltpu.make_async_copy(ref, ref, sem).wait()

    def span(start, size):
        return pl.ds(pl.multiple_of(start, size), size)

    barrier = pltpu.get_barrier_semaphore()

    def greet(device):
        pl.semaphore_signal(barrier, inc=1, device_id=device, device_id_type=MESH)

    for j in range(1, NC):
        greet((pr, rem(pc + j, NC)))
    for j in range(1, NX):
        greet(at_xz(rem(x + j, NX), z))
    greet(z_down)
    greet(z_up)
    rows = BLK * NSUP * S // 128
    blocks = [part * 4 + 2 * c + b for c in (core, 1 - core) for part in range(2) for b in range(2)]
    l_copies = [
        pltpu.make_async_copy(l_hbm.at[span(i * rows, rows)], lst.at[span(i * rows, rows)], l_sem.at[n])
        for n, i in enumerate(blocks)
    ]
    structure_copy = pltpu.make_async_copy(structure_hbm, structure, structure_sem)
    structure_copy.start()
    for copy in l_copies:
        copy.start()
    piv_copy = pltpu.make_async_copy(piv_hbm, piv, piv_sem)
    piv_copy.start()
    pl.semaphore_wait(barrier, NC - 1 + NX - 1 + 2)

    def a_piece(q, h):
        src = a_hbm.at[span(q * 32 + h * 16, 16)]
        return src, mid.at[pl.ds(h * 16, 16), span(pc * 256, 256)], m_recv.at[h, div(pc, 4)]

    for h in range(2):
        pltpu.make_async_copy(*a_piece(pc, h)).start()

        @pl.loop(1, NC)
        def _(j):
            q = rem(pc + j, NC)
            src, dst, recv = a_piece(q, h)
            remote(src, dst, m_send, recv, (pr, q)).start()

    structure_copy.wait()
    for copy in l_copies[:4]:
        copy.wait()

    def pack(j):
        for part in range(2):
            for b in range(2):
                i = part * 4 + 2 * core + b
                mask = structure[other, pr * NR + i].astype(F32)
                for col in range(W // 128):
                    first = i * rows + (j * (W // 128) + col) * NSUP + other
                    v = lst[pl.ds(first, BLK, stride=S * NSUP // 128), :]
                    xs[pl.ds(part * 128 + b * BLK, BLK), span((j * (W // 128) + col) * 128, 128)] = v * mask

    def x_copies(j, half):
        cols = span(j * W + half * H, H)
        return [
            remote(
                xs.at[pl.ds(part * 128, 128), cols],
                xin.at[span(part * 256 + core * 128, 128), cols],
                x_send, x_recv.at[part, 2 * j + half], device,
            )
            for part, device in enumerate((z_up, z_down))
        ]

    def send_x(j):
        for half in range(2):
            for copy in x_copies(j, half):
                copy.start()

    def p_copies(j, half):
        cols = span(j * W + half * H, H)
        return [
            remote(
                xin.at[span(part * 256 + core * 128, 128), cols],
                xin.at[span(part * 256 + core * 128, 128), cols],
                p_send, p_recv.at[part, 2 * j + half], partner,
            )
            for part in range(2)
        ]

    def relay(j, half, pass_on):
        cols = span(j * W + half * H, H)
        for part, (arrived, copy) in enumerate(zip(x_copies(j, half), p_copies(j, half))):
            arrived.wait_recv()
            if pass_on:
                block = xin.at[span(part * 256 + core * 128, 128), cols]
                remote(block, block, w_send, x_recv.at[part, 2 * j + half], (y_up, y_down)[part]).start()
            copy.start()

    def take(j):
        for half in range(2):
            for copy in p_copies(j, half):
                copy.wait_recv()
        cols = span(j * W, W)
        hi, lo = split(xin[:, cols])
        xhi[span(other * PART, PART), cols] = hi
        xlo[span(other * PART, PART), cols] = lo

    def prepare(i):
        mask = structure[zl, pr * NR + i].astype(F32)
        for col in range(S // 128):
            v = lst[pl.ds(i * rows + col * NSUP + zl, BLK, stride=S * NSUP // 128), :] * mask
            hi, lo = split(v)
            block = span(zl * PART + i * BLK, BLK)
            xhi[block, pl.ds(col * 128, 128)] = hi
            xlo[block, pl.ds(col * 128, 128)] = lo

    def forward(h):
        for j in (1, 2, 3, 0):
            xx = rem(x + j, NX)
            src = mid.at[pl.ds(h * 16, 16), span(xx * DEPTH, DEPTH)]
            await_bytes(src, m_recv.at[h, xx])
            dst, recv = abuf.at[0, span(x * 32 + h * 16, 16)], a_recv.at[h, x]
            if j:
                remote(src, dst, a_send, recv, at_xz(xx, z)).start()
            else:
                pltpu.make_async_copy(src, dst, recv).start()

    def share(h):
        for j in (0, 1, 3, 2):
            xx = rem(x + j, NX)
            block = span(xx * 32 + h * 16, 16)
            await_bytes(abuf.at[0, block], a_recv.at[h, xx])
            remote(abuf.at[0, block], abuf.at[1, block], n_send, n_recv, (z_up, z_down)[h]).start()

    def split_rows(g):
        hi, lo = split(abuf[g])
        ahi[g] = hi
        alo[g] = lo

    for n in (0, 2):
        pack(chunk(n))
        send_x(chunk(n))

    for copy in l_copies[4:]:
        copy.wait()

    @pl.loop(0, EARLY)
    def _(i):
        prepare(i)

    forward(0)

    @pl.loop(EARLY, NR)
    def _(i):
        prepare(i)

    forward(1)
    share(0)
    relay(chunk(0), 0, True)
    share(1)
    relay(chunk(0), 1, True)
    split_rows(0)

    def x_stage(buf, far, final, far_send, far_recv, final_send, final_recv):
        def first(j):
            cols = span(j * W, W)
            return [
                remote(
                    buf.at[span(x_far * 32 + h * 16, 16), cols],
                    far.at[h, :, cols], far_send, far_recv.at[h, j], device,
                )
                for h, device in enumerate((right, left))
            ]

        def second(j):
            cols = span(j * W, W)
            return [
                remote(
                    buf.at[span(target * 32, 32), cols],
                    final.at[h, :, cols], final_send, final_recv.at[h, j], device,
                )
                for h, (device, target) in enumerate(((right, x_next), (left, x_prev)))
            ]

        def send_first(j):
            for copy in first(j):
                copy.start()

        def send_second(j):
            cols = span(j * W, W)
            for h, (copy, target) in enumerate(zip(first(j), (x_next, x_prev))):
                copy.wait_recv()
                buf[span(target * 32 + h * 16, 16), cols] += far[h, :, cols]
            for copy in second(j):
                copy.start()

        def total(j):
            cols = span(j * W, W)
            for copy in second(j):
                copy.wait_recv()
            return buf[span(x * 32, 32), cols] + (final[0, :, cols] + final[1, :, cols])

        return send_first, send_second, total

    y_first, y_second, y_total = x_stage(ybuf, xo, xf, xo_send, xo_recv, xf_send, xf_recv)
    d_first, d_second, d_total = x_stage(dbuf, dxo, dxf, dxo_send, dxo_recv, dxf_send, dxf_recv)

    def item(i):
        own = i < 3 or i == 5
        n = (2 * i) % 3 if i < 3 else i - 3 if i < 5 else 3 if i == 5 else i - 4
        g, c = (0 if own else 1), chunk(n)
        return g, c, g * NCH + c

    def first_product(i):
        g, c, j = item(i)
        cols = span(c * W, W)
        ybuf[:, span(j * W, W)] = dot3(ahi[g], alo[g], xhi[:, cols], xlo[:, cols])
        y_first(j)

    def finish_c(i):
        g, c, j = item(i)
        cols = span(j * W, W)
        value = y_total(j)
        for h, neighbour in enumerate((z_down, z_up)):
            owner_row, owner_col = (pr, pc) if g == 0 else neighbour
            mask = structure[zl, owner_row * NR + div(owner_col, 2)].astype(F32)
            part = pl.ds(h * 16, 16)
            crow[part, cols] = -mask * value[h * 16 : h * 16 + 16]
            home = span(rem(owner_row, 2) * PART + owner_col * 32 + h * 16, 16)
            for n in range(W // T):
                q = (n // 2) * 8 + ((n % 2) * 2 + rem(c + n // 2, 2)) * 2 + div(c, 2)
                src = crow.at[part, span(j * W + n * T, T)]

                @pl.when(q == pc)
                def _():
                    pltpu.make_async_copy(src, cbuf.at[home], c_recv.at[g]).start()

                @pl.when(q != pc)
                def _():
                    remote(src, cbuf.at[home], c_send, c_recv.at[g], (pr, q)).start()

            if g == 1:
                remote(crow.at[part, cols], cout.at[part, span(c * W, W)], o_send, o_recv, neighbour).start()

        if g == 0:
            for n in range(W // 128):
                place = pl.ds((c * (W // 128) + n) * NSUP + zl, 32, stride=NSUP * S // 128)
                out_c[place, :] = crow[:, span(j * W + n * 128, 128)]

    owner_x = 2 * core + rem(y + zh, 2)
    owner = owner_x * 2 + zh

    def tile_y(target):
        return rem(y + 6 - owner_x + target, 4)

    def second_product(g):
        block = span((zl if g == 0 else other) * PART, PART)
        await_bytes(cbuf.at[block], c_recv.at[g])
        chi, clo = split(cbuf[block, :].T)
        for d in (2, 1, 3, 0):
            target = rem(x + d, NX)
            for b in range(2):
                cols = span(b * (S // 2) + tile_y(target) * 256, 256)
                value = dot3(chi, clo, xhi[block, cols], xlo[block, cols])
                for u in range(NCH):
                    part = span(target * 32, 32), pl.ds(u * W + b * 256, 256)
                    if g == 0:
                        dbuf[part] = value[u * 32 : u * 32 + 32]
                    else:
                        dbuf[part] += value[u * 32 : u * 32 + 32]
            if g == 1 and d == 2:
                for u in range(NCH):
                    d_first(u)

    def second_ring():
        @pl.loop(0, NCH)
        def _(n):
            d_second(n)

    def pass_on(n, onward):
        for half in range(2):
            relay(chunk(n), half, onward)

    take(chunk(0))
    first_product(0)
    pass_on(2, True)
    y_second(item(0)[2])
    pass_on(1, False)
    take(chunk(2))
    first_product(1)
    take(chunk(1))
    first_product(2)
    y_second(item(1)[2])
    finish_c(0)
    await_bytes(abuf.at[1], n_recv)
    split_rows(1)
    first_product(3)
    y_second(item(2)[2])
    pass_on(3, False)

    first_product(4)
    take(chunk(3))
    first_product(5)
    y_second(item(3)[2])
    first_product(6)
    first_product(7)
    y_second(item(4)[2])
    y_second(item(5)[2])
    finish_c(1)
    finish_c(2)
    y_second(item(6)[2])
    finish_c(3)
    y_second(item(7)[2])
    finish_c(4)
    finish_c(5)
    finish_c(6)
    finish_c(7)
    second_product(0)
    second_product(1)
    second_ring()

    @pl.loop(0, NCH)
    def _(u):
        dsum[:, span(u * W, W)] = d_total(u)
        for n in range(W // T):
            q = (n // 2) * 8 + tile_y(x) * 2 + n % 2
            src = dsum.at[:, span(u * W + n * T, T)]
            dst = dfin.at[zl, span(div(y, 2) * 128 + u * 32, 32)]
            remote(src, dst, d_send, d_recv, (owner, q)).start()

    await_bytes(cout, o_recv)
    for n in range(S // 128):
        out_c[pl.ds(n * NSUP + other, 32, stride=NSUP * S // 128), :] = cout[:, pl.ds(n * 128, 128)]
    await_bytes(abuf.at[0, pl.ds(0, 120)], m_send)
    await_bytes(abuf.at[0, pl.ds(0, 96)], a_send)
    await_bytes(abuf.at[0], n_send)
    await_bytes(xs.at[pl.ds(0, 128)], x_send)
    await_bytes(xs.at[pl.ds(0, 128)], w_send)
    await_bytes(xs, p_send)
    await_bytes(xo, xo_send)
    await_bytes(xf, xf_send)
    await_bytes(cbuf.at[pl.ds(0, 960)], c_send)
    await_bytes(cout, o_send)
    await_bytes(dxo, dxo_send)
    await_bytes(dxf, dxf_send)
    await_bytes(cbuf.at[pl.ds(0, 512)], d_send)

    piv_copy.wait()
    await_bytes(dfin, d_recv)
    for k in range(NSUP):
        out_d[k] = piv[k] - dfin[k].T


def place(columns, diagonal, out_c, out_d, sem):
    copies = [
        pltpu.make_async_copy(columns, out_c, sem.at[0]),
        pltpu.make_async_copy(diagonal, out_d, sem.at[1]),
    ]
    for copy in copies:
        copy.start()
    for copy in copies:
        copy.wait()


def body(ancestor_inverse, lower_panel, pivot_inverse, structure):
    panel = lower_panel.reshape(PART, NSUP, S // 128, 128).transpose(0, 2, 1, 3)
    panel = panel.reshape(PART * NSUP * S // 128, 128)
    width = NSUP * S
    vmem = pl.BlockSpec(memory_space=pltpu.VMEM)
    hbm = pl.BlockSpec(memory_space=pltpu.HBM)
    dma = pltpu.SemaphoreType.DMA
    columns, diagonal = pl.pallas_call(
        kernel,
        name="selinv",
        out_shape=(
            jax.ShapeDtypeStruct((32 * width // 128, 128), F32),
            jax.ShapeDtypeStruct(pivot_inverse.shape, F32),
        ),
        in_specs=[hbm, hbm, hbm, hbm],
        out_specs=(vmem, vmem),
        scratch_shapes=[
            pltpu.VMEM(pivot_inverse.shape, F32),
            pltpu.SMEM(structure.shape, structure.dtype),
            pltpu.VMEM(panel.shape, F32),
            pltpu.VMEM((256, S), F32),
            pltpu.VMEM((PART, S), F32),
            pltpu.VMEM((DEPTH, S), BF16),
            pltpu.VMEM((DEPTH, S), BF16),
            pltpu.VMEM((32, NX * DEPTH), F32),
            pltpu.VMEM((2, 128, DEPTH), F32),
            pltpu.VMEM((2, 128, DEPTH), BF16),
            pltpu.VMEM((2, 128, DEPTH), BF16),
            pltpu.VMEM((128, width), F32),
            pltpu.VMEM((2, 16, width), F32),
            pltpu.VMEM((2, 32, width), F32),
            pltpu.VMEM((32, width), F32),
            pltpu.VMEM((32, S), F32),
            pltpu.VMEM((DEPTH, T), F32),
            pltpu.VMEM((128, S), F32),
            pltpu.VMEM((2, 16, S), F32),
            pltpu.VMEM((2, 32, S), F32),
            pltpu.VMEM((32, S), F32),
            pltpu.VMEM((NSUP, 256, 128), F32),
            dma(()),
            dma(()),
            dma((NR,)),
            dma(()),
            dma((2, NX)),
            dma(()),
            dma((2, NX)),
            dma(()),
            dma(()),
            dma(()),
            dma((2, 2 * NCH)),
            dma(()),
            dma(()),
            dma((2, 2 * NCH)),
            dma(()),
            dma((2, ITEMS)),
            dma(()),
            dma((2, ITEMS)),
            dma(()),
            dma((2,)),
            dma(()),
            dma(()),
            dma(()),
            dma((2, NCH)),
            dma(()),
            dma((2, NCH)),
            dma(()),
            dma(()),
        ],
        compiler_params=pltpu.CompilerParams(
            collective_id=0, has_side_effects=True, vmem_limit_bytes=40 * 2**20
        ),
    )(
        *(
            pltpu.with_memory_space_constraint(v, pltpu.HBM)
            for v in (ancestor_inverse, panel, pivot_inverse, structure)
        )
    )
    columns, diagonal = pl.pallas_call(
        place,
        name="place",
        out_shape=(
            jax.ShapeDtypeStruct(columns.shape, F32),
            jax.ShapeDtypeStruct(diagonal.shape, F32),
        ),
        in_specs=[vmem, vmem],
        out_specs=(hbm, hbm),
        scratch_shapes=[dma((2,))],
        compiler_params=pltpu.CompilerParams(vmem_limit_bytes=2**20),
    )(columns, diagonal)
    columns = columns.reshape(32, S // 128, NSUP, 128).transpose(0, 2, 1, 3)
    return columns.reshape(32, NSUP, S), diagonal


def solution(mesh):
    return jax.shard_map(
        body,
        mesh=mesh,
        in_specs=(P("prow", "pcol"), P("prow", None, None), P(None, "pcol", "prow"), P()),
        out_specs=(P(("prow", "pcol"), None, None), P(None, "pcol", "prow")),
        check_vma=False,
    )
```

```python
import functools

import jax
import jax.numpy as jnp
from jax import lax
from jax.experimental import pallas as pl
from jax.experimental.pallas import tpu as pltpu
from jax.sharding import PartitionSpec as P

MESH = pl.DeviceIdType.MESH
F32 = jnp.float32
BF16 = jnp.bfloat16
S = 2048
NSUP = 2
BLK = 64
NX, NZ = 4, 4
NR, NC = 8, 16
PART = 512
DEPTH = 2 * PART
W = 512
NCH = S // W
ITEMS = 2 * NCH
EARLY = 5
H = W // 2
T = S // NC


def split(v):
    hi = v.astype(BF16)
    return hi, (v - hi.astype(F32)).astype(BF16)


def dot3(ahi, alo, bhi, blo):
    dot = functools.partial(jnp.dot, preferred_element_type=F32)
    return dot(ahi, bhi) + (dot(ahi, blo) + dot(alo, bhi))


def kernel(
    a_hbm, l_hbm, piv_hbm, structure_hbm, out_c, out_d,
    piv, structure, lst, xs, xin, xhi, xlo, mid, abuf, ahi, alo, ybuf, xo, xf,
    crow, cout, cbuf, dbuf, dxo, dxf, dsum, dfin,
    piv_sem, structure_sem, l_sem, m_send, m_recv, a_send, a_recv, n_send, n_recv,
    x_send, x_recv, w_send, p_send, p_recv, xo_send, xo_recv, xf_send, xf_recv,
    c_send, c_recv, o_send, o_recv, dxo_send, dxo_recv, dxf_send, dxf_recv, d_send, d_recv,
):
    rem, div = lax.rem, lax.div
    pr, pc = lax.axis_index("prow"), lax.axis_index("pcol")
    x, zl = div(pr, 2), rem(pr, 2)
    zh, rest = div(pc, 8), rem(pc, 8)
    y, core = div(rest, 2), rem(pc, 2)
    z = 2 * zh + zl
    other = 1 - zl

    def at_xz(xx, zz):
        return (xx * 2 + rem(zz, 2), div(zz, 2) * 8 + rest)

    z_down, z_up = at_xz(x, rem(z + 3, 4)), at_xz(x, rem(z + 1, 4))
    x_next, x_prev, x_far = rem(x + 1, 4), rem(x + 3, 4), rem(x + 2, 4)
    right, left = at_xz(x_next, z), at_xz(x_prev, z)
    partner = (pr, pc + 1 - 2 * core)
    y_up, y_down = ((pr, zh * 8 + rem(y + d, 4) * 2 + core) for d in (1, 3))
    parity = rem(y, 2)

    def chunk(n):
        return n + parity * (1 - 2 * rem(n, 2))

    def remote(src, dst, send, recv, device):
        return pltpu.make_async_remote_copy(
            src_ref=src, dst_ref=dst, send_sem=send, recv_sem=recv,
            device_id=device, device_id_type=MESH,
        )

    def await_bytes(ref, sem):
        pltpu.make_async_copy(ref, ref, sem).wait()

    def span(start, size):
        return pl.ds(pl.multiple_of(start, size), size)

    barrier = pltpu.get_barrier_semaphore()

    def greet(device):
        pl.semaphore_signal(barrier, inc=1, device_id=device, device_id_type=MESH)

    for j in range(1, NC):
        greet((pr, rem(pc + j, NC)))
    for j in range(1, NX):
        greet(at_xz(rem(x + j, NX), z))
    greet(z_down)
    greet(z_up)
    rows = BLK * NSUP * S // 128
    blocks = [part * 4 + 2 * c + b for c in (core, 1 - core) for part in range(2) for b in range(2)]
    l_copies = [
        pltpu.make_async_copy(l_hbm.at[span(i * rows, rows)], lst.at[span(i * rows, rows)], l_sem.at[n])
        for n, i in enumerate(blocks)
    ]
    structure_copy = pltpu.make_async_copy(structure_hbm, structure, structure_sem)
    structure_copy.start()
    for copy in l_copies:
        copy.start()
    piv_copy = pltpu.make_async_copy(piv_hbm, piv, piv_sem)
    piv_copy.start()
    pl.semaphore_wait(barrier, NC - 1 + NX - 1 + 2)

    def a_piece(q, h):
        src = a_hbm.at[span(q * 32 + h * 16, 16)]
        return src, mid.at[pl.ds(h * 16, 16), span(pc * 256, 256)], m_recv.at[h, div(pc, 4)]

    for h in range(2):
        pltpu.make_async_copy(*a_piece(pc, h)).start()

        @pl.loop(1, NC)
        def _(j):
            q = rem(pc + j, NC)
            src, dst, recv = a_piece(q, h)
            remote(src, dst, m_send, recv, (pr, q)).start()

    structure_copy.wait()
    for copy in l_copies[:4]:
        copy.wait()

    def pack(j):
        for part in range(2):
            for b in range(2):
                i = part * 4 + 2 * core + b
                mask = structure[other, pr * NR + i].astype(F32)
                for col in range(W // 128):
                    first = i * rows + (j * (W // 128) + col) * NSUP + other
                    v = lst[pl.ds(first, BLK, stride=S * NSUP // 128), :]
                    xs[pl.ds(part * 128 + b * BLK, BLK), span((j * (W // 128) + col) * 128, 128)] = v * mask

    def x_copies(j, half):
        cols = span(j * W + half * H, H)
        return [
            remote(
                xs.at[pl.ds(part * 128, 128), cols],
                xin.at[span(part * 256 + core * 128, 128), cols],
                x_send, x_recv.at[part, 2 * j + half], device,
            )
            for part, device in enumerate((z_up, z_down))
        ]

    def send_x(j):
        for half in range(2):
            for copy in x_copies(j, half):
                copy.start()

    def p_copies(j, half):
        cols = span(j * W + half * H, H)
        return [
            remote(
                xin.at[span(part * 256 + core * 128, 128), cols],
                xin.at[span(part * 256 + core * 128, 128), cols],
                p_send, p_recv.at[part, 2 * j + half], partner,
            )
            for part in range(2)
        ]

    def relay(j, half, pass_on):
        cols = span(j * W + half * H, H)
        for part, (arrived, copy) in enumerate(zip(x_copies(j, half), p_copies(j, half))):
            arrived.wait_recv()
            if pass_on:
                block = xin.at[span(part * 256 + core * 128, 128), cols]
                remote(block, block, w_send, x_recv.at[part, 2 * j + half], (y_up, y_down)[part]).start()
            copy.start()

    def take(j):
        for half in range(2):
            for copy in p_copies(j, half):
                copy.wait_recv()
        cols = span(j * W, W)
        hi, lo = split(xin[:, cols])
        xhi[span(other * PART, PART), cols] = hi
        xlo[span(other * PART, PART), cols] = lo

    def prepare(i):
        mask = structure[zl, pr * NR + i].astype(F32)
        for col in range(S // 128):
            v = lst[pl.ds(i * rows + col * NSUP + zl, BLK, stride=S * NSUP // 128), :] * mask
            hi, lo = split(v)
            block = span(zl * PART + i * BLK, BLK)
            xhi[block, pl.ds(col * 128, 128)] = hi
            xlo[block, pl.ds(col * 128, 128)] = lo

    def forward(h):
        for j in (1, 2, 3, 0):
            xx = rem(x + j, NX)
            src = mid.at[pl.ds(h * 16, 16), span(xx * DEPTH, DEPTH)]
            await_bytes(src, m_recv.at[h, xx])
            dst, recv = abuf.at[0, span(x * 32 + h * 16, 16)], a_recv.at[h, x]
            if j:
                remote(src, dst, a_send, recv, at_xz(xx, z)).start()
            else:
                pltpu.make_async_copy(src, dst, recv).start()

    def share(h):
        for j in (0, 1, 3, 2):
            xx = rem(x + j, NX)
            block = span(xx * 32 + h * 16, 16)
            await_bytes(abuf.at[0, block], a_recv.at[h, xx])
            remote(abuf.at[0, block], abuf.at[1, block], n_send, n_recv, (z_up, z_down)[h]).start()

    def split_rows(g):
        hi, lo = split(abuf[g])
        ahi[g] = hi
        alo[g] = lo

    for n in (0, 2):
        pack(chunk(n))
        send_x(chunk(n))

    for copy in l_copies[4:]:
        copy.wait()

    @pl.loop(0, EARLY)
    def _(i):
        prepare(i)

    forward(0)

    @pl.loop(EARLY, NR)
    def _(i):
        prepare(i)

    forward(1)
    relay(chunk(0), 0, True)
    share(0)
    relay(chunk(0), 1, True)
    share(1)
    split_rows(0)

    def x_stage(buf, far, final, far_send, far_recv, final_send, final_recv):
        def first(j):
            cols = span(j * W, W)
            return [
                remote(
                    buf.at[span(x_far * 32 + h * 16, 16), cols],
                    far.at[h, :, cols], far_send, far_recv.at[h, j], device,
                )
                for h, device in enumerate((right, left))
            ]

        def second(j):
            cols = span(j * W, W)
            return [
                remote(
                    buf.at[span(target * 32, 32), cols],
                    final.at[h, :, cols], final_send, final_recv.at[h, j], device,
                )
                for h, (device, target) in enumerate(((right, x_next), (left, x_prev)))
            ]

        def send_first(j):
            for copy in first(j):
                copy.start()

        def send_second(j):
            cols = span(j * W, W)
            for h, (copy, target) in enumerate(zip(first(j), (x_next, x_prev))):
                copy.wait_recv()
                buf[span(target * 32 + h * 16, 16), cols] += far[h, :, cols]
            for copy in second(j):
                copy.start()

        def total(j):
            cols = span(j * W, W)
            for copy in second(j):
                copy.wait_recv()
            return buf[span(x * 32, 32), cols] + (final[0, :, cols] + final[1, :, cols])

        return send_first, send_second, total

    y_first, y_second, y_total = x_stage(ybuf, xo, xf, xo_send, xo_recv, xf_send, xf_recv)
    d_first, d_second, d_total = x_stage(dbuf, dxo, dxf, dxo_send, dxo_recv, dxf_send, dxf_recv)

    def item(i):
        own = i < 3 or i == 5
        n = i if i < 3 else i - 3 if i < 5 else 3 if i == 5 else i - 4
        g, c = (0 if own else 1), chunk(n)
        return g, c, g * NCH + c

    def first_product(i):
        g, c, j = item(i)
        cols = span(c * W, W)
        ybuf[:, span(j * W, W)] = dot3(ahi[g], alo[g], xhi[:, cols], xlo[:, cols])
        y_first(j)

    def finish_c(i):
        g, c, j = item(i)
        cols = span(j * W, W)
        value = y_total(j)
        for h, neighbour in enumerate((z_down, z_up)):
            owner_row, owner_col = (pr, pc) if g == 0 else neighbour
            mask = structure[zl, owner_row * NR + div(owner_col, 2)].astype(F32)
            part = pl.ds(h * 16, 16)
            crow[part, cols] = -mask * value[h * 16 : h * 16 + 16]
            home = span(rem(owner_row, 2) * PART + owner_col * 32 + h * 16, 16)
            for n in range(W // T):
                q = (n // 2) * 8 + ((n % 2) * 2 + rem(c + n // 2, 2)) * 2 + div(c, 2)
                src = crow.at[part, span(j * W + n * T, T)]

                @pl.when(q == pc)
                def _():
                    pltpu.make_async_copy(src, cbuf.at[home], c_recv.at[g]).start()

                @pl.when(q != pc)
                def _():
                    remote(src, cbuf.at[home], c_send, c_recv.at[g], (pr, q)).start()

            if g == 1:
                remote(crow.at[part, cols], cout.at[part, span(c * W, W)], o_send, o_recv, neighbour).start()

        if g == 0:
            for n in range(W // 128):
                place = pl.ds((c * (W // 128) + n) * NSUP + zl, 32, stride=NSUP * S // 128)
                out_c[place, :] = crow[:, span(j * W + n * 128, 128)]

    owner_x = 2 * core + rem(y + zh, 2)
    owner = owner_x * 2 + zh

    def tile_y(target):
        return rem(y + 6 - owner_x + target, 4)

    def second_product(g):
        block = span((zl if g == 0 else other) * PART, PART)
        await_bytes(cbuf.at[block], c_recv.at[g])
        chi, clo = split(cbuf[block, :].T)
        for d in (2, 1, 3, 0):
            target = rem(x + d, NX)
            for b in range(2):
                cols = span(b * (S // 2) + tile_y(target) * 256, 256)
                value = dot3(chi, clo, xhi[block, cols], xlo[block, cols])
                for u in range(NCH):
                    part = span(target * 32, 32), pl.ds(u * W + b * 256, 256)
                    if g == 0:
                        dbuf[part] = value[u * 32 : u * 32 + 32]
                    else:
                        dbuf[part] += value[u * 32 : u * 32 + 32]
            if g == 1 and d == 2:
                for u in range(NCH):
                    d_first(u)

    def second_ring():
        @pl.loop(0, NCH)
        def _(n):
            d_second(n)

    take(chunk(0))
    first_product(0)
    relay(chunk(2), 0, True)
    relay(chunk(1), 0, False)
    relay(chunk(1), 1, False)
    y_second(item(0)[2])
    relay(chunk(2), 1, True)
    take(chunk(1))
    first_product(1)
    take(chunk(2))
    first_product(2)
    y_second(item(1)[2])
    finish_c(0)
    for half in range(2):
        relay(chunk(3), half, False)
    await_bytes(abuf.at[1], n_recv)
    split_rows(1)
    first_product(3)
    y_second(item(2)[2])

    first_product(4)
    take(chunk(3))
    first_product(5)
    y_second(item(3)[2])
    first_product(6)
    first_product(7)
    y_second(item(4)[2])
    y_second(item(5)[2])
    finish_c(1)
    finish_c(2)
    y_second(item(6)[2])
    finish_c(3)
    y_second(item(7)[2])
    finish_c(4)
    finish_c(5)
    finish_c(6)
    finish_c(7)
    second_product(0)
    second_product(1)
    second_ring()

    @pl.loop(0, NCH)
    def _(u):
        dsum[:, span(u * W, W)] = d_total(u)
        for n in range(W // T):
            q = (n // 2) * 8 + tile_y(x) * 2 + n % 2
            src = dsum.at[:, span(u * W + n * T, T)]
            dst = dfin.at[zl, span(div(y, 2) * 128 + u * 32, 32)]
            remote(src, dst, d_send, d_recv, (owner, q)).start()

    await_bytes(cout, o_recv)
    for n in range(S // 128):
        out_c[pl.ds(n * NSUP + other, 32, stride=NSUP * S // 128), :] = cout[:, pl.ds(n * 128, 128)]
    await_bytes(abuf.at[0, pl.ds(0, 120)], m_send)
    await_bytes(abuf.at[0, pl.ds(0, 96)], a_send)
    await_bytes(abuf.at[0], n_send)
    await_bytes(xs.at[pl.ds(0, 128)], x_send)
    await_bytes(xs.at[pl.ds(0, 128)], w_send)
    await_bytes(xs, p_send)
    await_bytes(xo, xo_send)
    await_bytes(xf, xf_send)
    await_bytes(cbuf.at[pl.ds(0, 960)], c_send)
    await_bytes(cout, o_send)
    await_bytes(dxo, dxo_send)
    await_bytes(dxf, dxf_send)
    await_bytes(cbuf.at[pl.ds(0, 512)], d_send)

    piv_copy.wait()
    await_bytes(dfin, d_recv)
    for k in range(NSUP):
        out_d[k] = piv[k] - dfin[k].T


def place(columns, diagonal, out_c, out_d, sem):
    copies = [
        pltpu.make_async_copy(columns, out_c, sem.at[0]),
        pltpu.make_async_copy(diagonal, out_d, sem.at[1]),
    ]
    for copy in copies:
        copy.start()
    for copy in copies:
        copy.wait()


def body(ancestor_inverse, lower_panel, pivot_inverse, structure):
    panel = lower_panel.reshape(PART, NSUP, S // 128, 128).transpose(0, 2, 1, 3)
    panel = panel.reshape(PART * NSUP * S // 128, 128)
    width = NSUP * S
    vmem = pl.BlockSpec(memory_space=pltpu.VMEM)
    hbm = pl.BlockSpec(memory_space=pltpu.HBM)
    dma = pltpu.SemaphoreType.DMA
    columns, diagonal = pl.pallas_call(
        kernel,
        name="selinv",
        out_shape=(
            jax.ShapeDtypeStruct((32 * width // 128, 128), F32),
            jax.ShapeDtypeStruct(pivot_inverse.shape, F32),
        ),
        in_specs=[hbm, hbm, hbm, hbm],
        out_specs=(vmem, vmem),
        scratch_shapes=[
            pltpu.VMEM(pivot_inverse.shape, F32),
            pltpu.SMEM(structure.shape, structure.dtype),
            pltpu.VMEM(panel.shape, F32),
            pltpu.VMEM((256, S), F32),
            pltpu.VMEM((PART, S), F32),
            pltpu.VMEM((DEPTH, S), BF16),
            pltpu.VMEM((DEPTH, S), BF16),
            pltpu.VMEM((32, NX * DEPTH), F32),
            pltpu.VMEM((2, 128, DEPTH), F32),
            pltpu.VMEM((2, 128, DEPTH), BF16),
            pltpu.VMEM((2, 128, DEPTH), BF16),
            pltpu.VMEM((128, width), F32),
            pltpu.VMEM((2, 16, width), F32),
            pltpu.VMEM((2, 32, width), F32),
            pltpu.VMEM((32, width), F32),
            pltpu.VMEM((32, S), F32),
            pltpu.VMEM((DEPTH, T), F32),
            pltpu.VMEM((128, S), F32),
            pltpu.VMEM((2, 16, S), F32),
            pltpu.VMEM((2, 32, S), F32),
            pltpu.VMEM((32, S), F32),
            pltpu.VMEM((NSUP, 256, 128), F32),
            dma(()),
            dma(()),
            dma((NR,)),
            dma(()),
            dma((2, NX)),
            dma(()),
            dma((2, NX)),
            dma(()),
            dma(()),
            dma(()),
            dma((2, 2 * NCH)),
            dma(()),
            dma(()),
            dma((2, 2 * NCH)),
            dma(()),
            dma((2, ITEMS)),
            dma(()),
            dma((2, ITEMS)),
            dma(()),
            dma((2,)),
            dma(()),
            dma(()),
            dma(()),
            dma((2, NCH)),
            dma(()),
            dma((2, NCH)),
            dma(()),
            dma(()),
        ],
        compiler_params=pltpu.CompilerParams(
            collective_id=0, has_side_effects=True, vmem_limit_bytes=40 * 2**20
        ),
    )(
        *(
            pltpu.with_memory_space_constraint(v, pltpu.HBM)
            for v in (ancestor_inverse, panel, pivot_inverse, structure)
        )
    )
    columns, diagonal = pl.pallas_call(
        place,
        name="place",
        out_shape=(
            jax.ShapeDtypeStruct(columns.shape, F32),
            jax.ShapeDtypeStruct(diagonal.shape, F32),
        ),
        in_specs=[vmem, vmem],
        out_specs=(hbm, hbm),
        scratch_shapes=[dma((2,))],
        compiler_params=pltpu.CompilerParams(vmem_limit_bytes=2**20),
    )(columns, diagonal)
    columns = columns.reshape(32, S // 128, NSUP, 128).transpose(0, 2, 1, 3)
    return columns.reshape(32, NSUP, S), diagonal


def solution(mesh):
    return jax.shard_map(
        body,
        mesh=mesh,
        in_specs=(P("prow", "pcol"), P("prow", None, None), P(None, "pcol", "prow"), P()),
        out_specs=(P(("prow", "pcol"), None, None), P(None, "pcol", "prow")),
        check_vma=False,
    )
```

```python
import functools

import jax
import jax.numpy as jnp
from jax import lax
from jax.experimental import pallas as pl
from jax.experimental.pallas import tpu as pltpu
from jax.sharding import PartitionSpec as P

MESH = pl.DeviceIdType.MESH
F32 = jnp.float32
BF16 = jnp.bfloat16
S = 2048
NSUP = 2
BLK = 64
NX, NZ = 4, 4
NR, NC = 8, 16
PART = 512
DEPTH = 2 * PART
W = 512
NCH = S // W
ITEMS = 2 * NCH
EARLY = 5
H = W // 2
T = S // NC


def split(v):
    hi = v.astype(BF16)
    return hi, (v - hi.astype(F32)).astype(BF16)


def dot3(ahi, alo, bhi, blo):
    dot = functools.partial(jnp.dot, preferred_element_type=F32)
    return dot(ahi, bhi) + (dot(ahi, blo) + dot(alo, bhi))


def kernel(
    a_hbm, l_hbm, piv_hbm, structure_hbm, out_c, out_d,
    piv, structure, lst, xs, xin, xhi, xlo, mid, abuf, ahi, alo, ybuf, xo, xf,
    crow, cout, cbuf, dbuf, dxo, dxf, dsum, dfin,
    piv_sem, structure_sem, l_sem, m_send, m_recv, a_send, a_recv, n_send, n_recv,
    x_send, x_recv, w_send, p_send, p_recv, xo_send, xo_recv, xf_send, xf_recv,
    c_send, c_recv, o_send, o_recv, dxo_send, dxo_recv, dxf_send, dxf_recv, d_send, d_recv,
):
    rem, div = lax.rem, lax.div
    pr, pc = lax.axis_index("prow"), lax.axis_index("pcol")
    x, zl = div(pr, 2), rem(pr, 2)
    zh, rest = div(pc, 8), rem(pc, 8)
    y, core = div(rest, 2), rem(pc, 2)
    z = 2 * zh + zl
    other = 1 - zl

    def at_xz(xx, zz):
        return (xx * 2 + rem(zz, 2), div(zz, 2) * 8 + rest)

    z_down, z_up = at_xz(x, rem(z + 3, 4)), at_xz(x, rem(z + 1, 4))
    x_next, x_prev, x_far = rem(x + 1, 4), rem(x + 3, 4), rem(x + 2, 4)
    right, left = at_xz(x_next, z), at_xz(x_prev, z)
    partner = (pr, pc + 1 - 2 * core)
    y_up, y_down = ((pr, zh * 8 + rem(y + d, 4) * 2 + core) for d in (1, 3))
    parity = rem(y, 2)

    def chunk(n):
        return n + parity * (1 - 2 * rem(n, 2))

    def remote(src, dst, send, recv, device):
        return pltpu.make_async_remote_copy(
            src_ref=src, dst_ref=dst, send_sem=send, recv_sem=recv,
            device_id=device, device_id_type=MESH,
        )

    def await_bytes(ref, sem):
        pltpu.make_async_copy(ref, ref, sem).wait()

    def span(start, size):
        return pl.ds(pl.multiple_of(start, size), size)

    barrier = pltpu.get_barrier_semaphore()

    def greet(device):
        pl.semaphore_signal(barrier, inc=1, device_id=device, device_id_type=MESH)

    for j in range(1, NC):
        greet((pr, rem(pc + j, NC)))
    for j in range(1, NX):
        greet(at_xz(rem(x + j, NX), z))
    greet(z_down)
    greet(z_up)
    rows = BLK * NSUP * S // 128
    blocks = [part * 4 + 2 * c + b for c in (core, 1 - core) for part in range(2) for b in range(2)]
    l_copies = [
        pltpu.make_async_copy(l_hbm.at[span(i * rows, rows)], lst.at[span(i * rows, rows)], l_sem.at[n])
        for n, i in enumerate(blocks)
    ]
    structure_copy = pltpu.make_async_copy(structure_hbm, structure, structure_sem)
    structure_copy.start()
    for copy in l_copies:
        copy.start()
    piv_copy = pltpu.make_async_copy(piv_hbm, piv, piv_sem)
    piv_copy.start()
    pl.semaphore_wait(barrier, NC - 1 + NX - 1 + 2)

    def a_piece(q, h):
        src = a_hbm.at[span(q * 32 + h * 16, 16)]
        return src, mid.at[pl.ds(h * 16, 16), span(pc * 256, 256)], m_recv.at[h, div(pc, 4)]

    for h in range(2):
        pltpu.make_async_copy(*a_piece(pc, h)).start()

        @pl.loop(1, NC)
        def _(j):
            q = rem(pc + j, NC)
            src, dst, recv = a_piece(q, h)
            remote(src, dst, m_send, recv, (pr, q)).start()

    structure_copy.wait()
    for copy in l_copies[:4]:
        copy.wait()

    def pack(j):
        for part in range(2):
            for b in range(2):
                i = part * 4 + 2 * core + b
                mask = structure[other, pr * NR + i].astype(F32)
                for col in range(W // 128):
                    first = i * rows + (j * (W // 128) + col) * NSUP + other
                    v = lst[pl.ds(first, BLK, stride=S * NSUP // 128), :]
                    xs[pl.ds(part * 128 + b * BLK, BLK), span((j * (W // 128) + col) * 128, 128)] = v * mask

    def x_copies(j, half):
        cols = span(j * W + half * H, H)
        return [
            remote(
                xs.at[pl.ds(part * 128, 128), cols],
                xin.at[span(part * 256 + core * 128, 128), cols],
                x_send, x_recv.at[part, 2 * j + half], device,
            )
            for part, device in enumerate((z_up, z_down))
        ]

    def send_x(j):
        for half in range(2):
            for copy in x_copies(j, half):
                copy.start()

    def p_copies(j, half):
        cols = span(j * W + half * H, H)
        return [
            remote(
                xin.at[span(part * 256 + core * 128, 128), cols],
                xin.at[span(part * 256 + core * 128, 128), cols],
                p_send, p_recv.at[part, 2 * j + half], partner,
            )
            for part in range(2)
        ]

    def relay(j, half, pass_on):
        cols = span(j * W + half * H, H)
        for part, (arrived, copy) in enumerate(zip(x_copies(j, half), p_copies(j, half))):
            arrived.wait_recv()
            if pass_on:
                block = xin.at[span(part * 256 + core * 128, 128), cols]
                remote(block, block, w_send, x_recv.at[part, 2 * j + half], (y_up, y_down)[part]).start()
            copy.start()

    def take(j):
        for half in range(2):
            for copy in p_copies(j, half):
                copy.wait_recv()
        cols = span(j * W, W)
        hi, lo = split(xin[:, cols])
        xhi[span(other * PART, PART), cols] = hi
        xlo[span(other * PART, PART), cols] = lo

    def prepare(i):
        mask = structure[zl, pr * NR + i].astype(F32)
        for col in range(S // 128):
            v = lst[pl.ds(i * rows + col * NSUP + zl, BLK, stride=S * NSUP // 128), :] * mask
            hi, lo = split(v)
            block = span(zl * PART + i * BLK, BLK)
            xhi[block, pl.ds(col * 128, 128)] = hi
            xlo[block, pl.ds(col * 128, 128)] = lo

    def forward(h):
        for j in (1, 2, 3, 0):
            xx = rem(x + j, NX)
            src = mid.at[pl.ds(h * 16, 16), span(xx * DEPTH, DEPTH)]
            await_bytes(src, m_recv.at[h, xx])
            dst, recv = abuf.at[0, span(x * 32 + h * 16, 16)], a_recv.at[h, x]
            if j:
                remote(src, dst, a_send, recv, at_xz(xx, z)).start()
            else:
                pltpu.make_async_copy(src, dst, recv).start()

    def share(h):
        for j in (0, 1, 3, 2):
            xx = rem(x + j, NX)
            block = span(xx * 32 + h * 16, 16)
            await_bytes(abuf.at[0, block], a_recv.at[h, xx])
            remote(abuf.at[0, block], abuf.at[1, block], n_send, n_recv, (z_up, z_down)[h]).start()

    def split_rows(g):
        hi, lo = split(abuf[g])
        ahi[g] = hi
        alo[g] = lo

    for n in (0, 2):
        pack(chunk(n))
        send_x(chunk(n))

    for copy in l_copies[4:]:
        copy.wait()

    @pl.loop(0, EARLY)
    def _(i):
        prepare(i)

    forward(0)

    @pl.loop(EARLY, NR)
    def _(i):
        prepare(i)

    forward(1)
    relay(chunk(0), 0, True)
    share(0)
    relay(chunk(0), 1, True)
    share(1)
    split_rows(0)

    def x_stage(buf, far, final, far_send, far_recv, final_send, final_recv):
        def first(j):
            cols = span(j * W, W)
            return [
                remote(
                    buf.at[span(x_far * 32 + h * 16, 16), cols],
                    far.at[h, :, cols], far_send, far_recv.at[h, j], device,
                )
                for h, device in enumerate((right, left))
            ]

        def second(j):
            cols = span(j * W, W)
            return [
                remote(
                    buf.at[span(target * 32, 32), cols],
                    final.at[h, :, cols], final_send, final_recv.at[h, j], device,
                )
                for h, (device, target) in enumerate(((right, x_next), (left, x_prev)))
            ]

        def send_first(j):
            for copy in first(j):
                copy.start()

        def send_second(j):
            cols = span(j * W, W)
            for h, (copy, target) in enumerate(zip(first(j), (x_next, x_prev))):
                copy.wait_recv()
                buf[span(target * 32 + h * 16, 16), cols] += far[h, :, cols]
            for copy in second(j):
                copy.start()

        def total(j):
            cols = span(j * W, W)
            for copy in second(j):
                copy.wait_recv()
            return buf[span(x * 32, 32), cols] + (final[0, :, cols] + final[1, :, cols])

        return send_first, send_second, total

    y_first, y_second, y_total = x_stage(ybuf, xo, xf, xo_send, xo_recv, xf_send, xf_recv)
    d_first, d_second, d_total = x_stage(dbuf, dxo, dxf, dxo_send, dxo_recv, dxf_send, dxf_recv)

    def item(i):
        own = i < 3 or i == 5
        n = i if i < 3 else i - 3 if i < 5 else 3 if i == 5 else i - 4
        g, c = (0 if own else 1), chunk(n)
        return g, c, g * NCH + c

    def first_product(i):
        g, c, j = item(i)
        cols = span(c * W, W)
        ybuf[:, span(j * W, W)] = dot3(ahi[g], alo[g], xhi[:, cols], xlo[:, cols])
        y_first(j)

    def finish_c(i):
        g, c, j = item(i)
        cols = span(j * W, W)
        value = y_total(j)
        for h, neighbour in enumerate((z_down, z_up)):
            owner_row, owner_col = (pr, pc) if g == 0 else neighbour
            mask = structure[zl, owner_row * NR + div(owner_col, 2)].astype(F32)
            part = pl.ds(h * 16, 16)
            crow[part, cols] = -mask * value[h * 16 : h * 16 + 16]
            home = span(rem(owner_row, 2) * PART + owner_col * 32 + h * 16, 16)
            if g == 0 and h == 0:
                continue
            if g == 0:
                sent = pl.ds(0, 32)
                home = span(zl * PART + pc * 32, 32)
            else:
                sent = part
            for n in range(W // T):
                q = (n // 2) * 8 + ((n % 2) * 2 + rem(c + n // 2, 2)) * 2 + div(c, 2)
                src = crow.at[sent, span(j * W + n * T, T)]

                @pl.when(q == pc)
                def _():
                    pltpu.make_async_copy(src, cbuf.at[home], c_recv.at[g]).start()

                @pl.when(q != pc)
                def _():
                    remote(src, cbuf.at[home], c_send, c_recv.at[g], (pr, q)).start()

            if g == 1:
                remote(crow.at[part, cols], cout.at[part, span(c * W, W)], o_send, o_recv, neighbour).start()

        if g == 0:
            for n in range(W // 128):
                place = pl.ds((c * (W // 128) + n) * NSUP + zl, 32, stride=NSUP * S // 128)
                out_c[place, :] = crow[:, span(j * W + n * 128, 128)]

    owner_x = 2 * core + rem(y + zh, 2)
    owner = owner_x * 2 + zh

    def tile_y(target):
        return rem(y + 6 - owner_x + target, 4)

    def second_product(g):
        block = span((zl if g == 0 else other) * PART, PART)
        await_bytes(cbuf.at[block], c_recv.at[g])
        chi, clo = split(cbuf[block, :].T)
        for d in (2, 1, 3, 0):
            target = rem(x + d, NX)
            for b in range(2):
                cols = span(b * (S // 2) + tile_y(target) * 256, 256)
                value = dot3(chi, clo, xhi[block, cols], xlo[block, cols])
                for u in range(NCH):
                    part = span(target * 32, 32), pl.ds(u * W + b * 256, 256)
                    if g == 0:
                        dbuf[part] = value[u * 32 : u * 32 + 32]
                    else:
                        dbuf[part] += value[u * 32 : u * 32 + 32]
            if g == 1 and d == 2:
                for u in range(NCH):
                    d_first(u)

    def second_ring():
        @pl.loop(0, NCH)
        def _(n):
            d_second(n)

    take(chunk(0))
    first_product(0)
    relay(chunk(2), 0, True)
    relay(chunk(1), 0, False)
    relay(chunk(1), 1, False)
    y_second(item(0)[2])
    relay(chunk(2), 1, True)
    take(chunk(1))
    first_product(1)
    take(chunk(2))
    first_product(2)
    y_second(item(1)[2])
    finish_c(0)
    for half in range(2):
        relay(chunk(3), half, False)
    await_bytes(abuf.at[1], n_recv)
    split_rows(1)
    first_product(3)
    y_second(item(2)[2])

    first_product(4)
    take(chunk(3))
    first_product(5)
    first_product(6)
    y_second(item(3)[2])
    first_product(7)
    y_second(item(4)[2])
    y_second(item(5)[2])
    finish_c(1)
    finish_c(2)
    y_second(item(6)[2])
    finish_c(3)
    y_second(item(7)[2])
    finish_c(4)
    finish_c(5)
    finish_c(6)
    finish_c(7)
    second_product(0)
    second_product(1)
    second_ring()

    @pl.loop(0, NCH)
    def _(u):
        dsum[:, span(u * W, W)] = d_total(u)
        for n in range(W // T):
            q = (n // 2) * 8 + tile_y(x) * 2 + n % 2
            src = dsum.at[:, span(u * W + n * T, T)]
            dst = dfin.at[zl, span(div(y, 2) * 128 + u * 32, 32)]
            remote(src, dst, d_send, d_recv, (owner, q)).start()

    await_bytes(cout, o_recv)
    for n in range(S // 128):
        out_c[pl.ds(n * NSUP + other, 32, stride=NSUP * S // 128), :] = cout[:, pl.ds(n * 128, 128)]
    await_bytes(abuf.at[0, pl.ds(0, 120)], m_send)
    await_bytes(abuf.at[0, pl.ds(0, 96)], a_send)
    await_bytes(abuf.at[0], n_send)
    await_bytes(xs.at[pl.ds(0, 128)], x_send)
    await_bytes(xs.at[pl.ds(0, 128)], w_send)
    await_bytes(xs, p_send)
    await_bytes(xo, xo_send)
    await_bytes(xf, xf_send)
    await_bytes(cbuf.at[pl.ds(0, 960)], c_send)
    await_bytes(cout, o_send)
    await_bytes(dxo, dxo_send)
    await_bytes(dxf, dxf_send)
    await_bytes(cbuf.at[pl.ds(0, 512)], d_send)

    piv_copy.wait()
    await_bytes(dfin, d_recv)
    for k in range(NSUP):
        out_d[k] = piv[k] - dfin[k].T


def place(columns, diagonal, out_c, out_d, sem):
    copies = [
        pltpu.make_async_copy(columns, out_c, sem.at[0]),
        pltpu.make_async_copy(diagonal, out_d, sem.at[1]),
    ]
    for copy in copies:
        copy.start()
    for copy in copies:
        copy.wait()


def body(ancestor_inverse, lower_panel, pivot_inverse, structure):
    panel = lower_panel.reshape(PART, NSUP, S // 128, 128).transpose(0, 2, 1, 3)
    panel = panel.reshape(PART * NSUP * S // 128, 128)
    width = NSUP * S
    vmem = pl.BlockSpec(memory_space=pltpu.VMEM)
    hbm = pl.BlockSpec(memory_space=pltpu.HBM)
    dma = pltpu.SemaphoreType.DMA
    columns, diagonal = pl.pallas_call(
        kernel,
        name="selinv",
        out_shape=(
            jax.ShapeDtypeStruct((32 * width // 128, 128), F32),
            jax.ShapeDtypeStruct(pivot_inverse.shape, F32),
        ),
        in_specs=[hbm, hbm, hbm, hbm],
        out_specs=(vmem, vmem),
        scratch_shapes=[
            pltpu.VMEM(pivot_inverse.shape, F32),
            pltpu.SMEM(structure.shape, structure.dtype),
            pltpu.VMEM(panel.shape, F32),
            pltpu.VMEM((256, S), F32),
            pltpu.VMEM((PART, S), F32),
            pltpu.VMEM((DEPTH, S), BF16),
            pltpu.VMEM((DEPTH, S), BF16),
            pltpu.VMEM((32, NX * DEPTH), F32),
            pltpu.VMEM((2, 128, DEPTH), F32),
            pltpu.VMEM((2, 128, DEPTH), BF16),
            pltpu.VMEM((2, 128, DEPTH), BF16),
            pltpu.VMEM((128, width), F32),
            pltpu.VMEM((2, 16, width), F32),
            pltpu.VMEM((2, 32, width), F32),
            pltpu.VMEM((32, width), F32),
            pltpu.VMEM((32, S), F32),
            pltpu.VMEM((DEPTH, T), F32),
            pltpu.VMEM((128, S), F32),
            pltpu.VMEM((2, 16, S), F32),
            pltpu.VMEM((2, 32, S), F32),
            pltpu.VMEM((32, S), F32),
            pltpu.VMEM((NSUP, 256, 128), F32),
            dma(()),
            dma(()),
            dma((NR,)),
            dma(()),
            dma((2, NX)),
            dma(()),
            dma((2, NX)),
            dma(()),
            dma(()),
            dma(()),
            dma((2, 2 * NCH)),
            dma(()),
            dma(()),
            dma((2, 2 * NCH)),
            dma(()),
            dma((2, ITEMS)),
            dma(()),
            dma((2, ITEMS)),
            dma(()),
            dma((2,)),
            dma(()),
            dma(()),
            dma(()),
            dma((2, NCH)),
            dma(()),
            dma((2, NCH)),
            dma(()),
            dma(()),
        ],
        compiler_params=pltpu.CompilerParams(
            collective_id=0, has_side_effects=True, vmem_limit_bytes=40 * 2**20
        ),
    )(
        *(
            pltpu.with_memory_space_constraint(v, pltpu.HBM)
            for v in (ancestor_inverse, panel, pivot_inverse, structure)
        )
    )
    columns, diagonal = pl.pallas_call(
        place,
        name="place",
        out_shape=(
            jax.ShapeDtypeStruct(columns.shape, F32),
            jax.ShapeDtypeStruct(diagonal.shape, F32),
        ),
        in_specs=[vmem, vmem],
        out_specs=(hbm, hbm),
        scratch_shapes=[dma((2,))],
        compiler_params=pltpu.CompilerParams(vmem_limit_bytes=2**20),
    )(columns, diagonal)
    columns = columns.reshape(32, S // 128, NSUP, 128).transpose(0, 2, 1, 3)
    return columns.reshape(32, NSUP, S), diagonal


def solution(mesh):
    return jax.shard_map(
        body,
        mesh=mesh,
        in_specs=(P("prow", "pcol"), P("prow", None, None), P(None, "pcol", "prow"), P()),
        out_specs=(P(("prow", "pcol"), None, None), P(None, "pcol", "prow")),
        check_vma=False,
    )
```
